256 devices in a mesh: seq: 32 (over x, z), head: 8 (over y, core).
Axes of the slice: x: 4, y: 4, z: 8, core: 2. Of those that a mesh axis runs over, the one named last changes fastest.
Arguments:
- queries: bfloat16 [32768, 4096], P('seq', 'head'), may hold values from -0.23925781 to 0.23925781
- keys: bfloat16 [32768, 4096], P('seq', 'head'), may hold values from -0.23925781 to 0.23925781
- values: bfloat16 [32768, 4096], P('seq', 'head'), may hold values from -1.5 to 1.5
- out_grad: bfloat16 [32768, 4096], P('seq', 'head'), may hold values from -1.5 to 1.5
- starts: int32 [32768], P('seq'), may hold values 0 or 1
- owners: int32 [32768, 1], P('seq'), may hold values from 0 to 7; in each aligned block of 1024 rows (0 to 1023, 1024 to 2047, ...) at most 256 rows name the same one
Outputs:
- returned: bfloat16 [65536, 3, 4096], P(('seq', 'head'))
The draws below stay inside these ranges and needn't reach their ends.
Inputs may be any that keep to these rules, and one draw needn't show every extreme that they name: `owners`: among the 1024 tokens of one block, no owner is named by more than 256 tokens, a bound that some block reaches.
All inputs are finite; a program needn't handle non-finite values. No bound on the sum of `starts` on one device may be relied on, other than what follows from the above.
Results may differ from the reference program's by a relative error of at most 0.0049.
Values may be sent and summed in bfloat16 or wider, within the bound.
No kernel may reach another device: no remote copies, remote signals or barrier semaphores. Data moves between devices by JAX's collectives and lax.ppermute only.
A program may use at most 128 MiB of HBM per device.

```python
import math
import jax
import jax.numpy as jnp
import numpy as np
from jax import lax

HD = 128
H = 32
SPAN = 1024
TOKENS = 32768
CAP = 256
N_SEQ = 32
N_HEAD = 8


def plant(array, key, smallest, top_value):
    extent = array.shape
    place = [jax.random.randint(jax.random.fold_in(key, axis), (), 0, extent[axis]) for axis in range(len(extent))]
    array = array.at[tuple(place)].set(smallest)
    longest = extent.index(max(extent))
    place[longest] = (place[longest] + 1) % extent[longest]
    return array.at[tuple(place)].set(top_value)


def level_of(rng, shape, pieces, low, largest):
    factor_of, own = 1.0, jax.random.fold_in(rng, 6)
    for dim, blocks in pieces:
        steps = jnp.exp(jax.random.uniform(jax.random.fold_in(own, dim), (blocks,), jnp.float32, low / len(pieces), largest / len(pieces)))
        factor_of = factor_of * jnp.repeat(steps, shape[dim] // blocks).reshape([-1 if axis == dim else 1 for axis in range(len(shape))])
    return factor_of


def shared_out(own_key, own, number, rows, amount, top, bound, slope):
    order = jax.random.permutation(own_key, amount)
    packed, common = shares(amount, rows * top, bound, slope, True), shares(amount, rows * top, bound, slope, False)
    places = jnp.arange(amount)

    def named(lengths, turn):
        used = int((lengths > 0).sum())
        fixed = max(1, used // 4)
        shifted = fixed + (places - fixed + turn * (used - fixed)) % max(1, amount - fixed)
        return jnp.zeros((amount,), jnp.int32).at[order[jnp.where(places < fixed, places, shifted)]].set(jnp.asarray(lengths, jnp.int32))

    lengths = jnp.where(number % 4 == 0, named(packed, number // 4), named(common, number - number // 4 - 1))
    mixed = jax.random.permutation(jax.random.fold_in(own, 3), amount)
    donor, sink = mixed[0:amount // 2 * 2:2], mixed[1:amount // 2 * 2:2]
    room = jnp.minimum(lengths[donor] - 1, bound - lengths[sink]) // 2
    room = jnp.where((donor == order[0]) | (sink == order[0]) | (lengths[sink] == 0), 0, jnp.maximum(room, 0))
    shifted = jax.random.randint(jax.random.fold_in(own, 4), (amount // 2,), 0, 1 << 20) % (room + 1)
    lengths = lengths.at[donor].add(-shifted).at[sink].add(shifted)
    members = jnp.searchsorted(jnp.cumsum(lengths), jnp.arange(rows * top), side="right").astype(jnp.int32)
    grid = members.reshape(top, rows).T
    grid = grid[jax.random.permutation(jax.random.fold_in(own, 1), rows)]
    turn = jax.random.randint(jax.random.fold_in(own, 2), (rows, 1), 0, top)
    return jnp.take_along_axis(grid, (jnp.arange(top)[None, :] + turn) % top, axis=1)


def shares(number_of, total, limit, slope, full):
    portions = [(1 << 20) // math.isqrt(rank ** slope) + 1 for rank in range(1, number_of + 1)]
    largest = limit if full else min(limit, max(-(-total // number_of), total * portions[0] // sum(portions)))
    least = 1 if total - largest >= number_of - 1 else 0
    given, rest = [largest] + [least] * (number_of - 1), total - largest - least * (number_of - 1)
    while rest > 0:
        free = [i for i in range(1, number_of) if given[i] < largest] or [i for i in range(1, number_of) if given[i] < limit]
        whole, budget = sum([portions[i] for i in free]), rest
        for i in free:
            more = min(limit - given[i], max(1, budget * portions[i] // whole), rest)
            given[i] = given[i] + more
            rest = rest - more
    return np.array(given)


def bell_draw(rng, extent, scale, reach, pieces=(), kind=jnp.bfloat16):
    drawn = scale * jax.random.normal(rng, extent, jnp.float32)
    if pieces:
        drawn = drawn * level_of(rng, extent, pieces, -0.22, 0.18)
    return jnp.clip(drawn, -reach, reach).astype(kind)


def setup_inputs(seed: int = 0) -> dict:
    arg_keys = jax.random.split(jax.random.key(seed), 7)
    queries = bell_draw(arg_keys[0], (TOKENS, H * HD), 0.04, 0.23925781, ((0, 32), (1, 8)))
    keys = bell_draw(arg_keys[1], (TOKENS, H * HD), 0.04, 0.23925781, ((0, 32), (1, 8)))
    values = bell_draw(arg_keys[2], (TOKENS, H * HD), 0.25, 1.5, ((0, 32), (1, 8)))
    out_grad = bell_draw(arg_keys[3], (TOKENS, H * HD), 0.25, 1.5, ((0, 32), (1, 8)))
    starts = plant((jax.random.randint(arg_keys[4], (TOKENS,), 0, 4 * SPAN) < 1).astype(jnp.int32), jax.random.fold_in(arg_keys[4], 1), 0, 1)
    owners_keys = jax.random.split(jax.random.fold_in(arg_keys[5], 1), TOKENS // SPAN)
    owners_turns = jax.random.permutation(jax.random.fold_in(arg_keys[5], 3), TOKENS // SPAN)
    owners = jax.vmap(lambda own, number: shared_out(jax.random.fold_in(arg_keys[5], 2), own, number, SPAN, N_HEAD, 1, CAP, 2))(owners_keys, owners_turns).reshape((TOKENS, 1))
    return {"queries": queries, "keys": keys, "values": values, "out_grad": out_grad, "starts": starts, "owners": owners}


def block_states(item):
    queries, keys, values, out_grad, starts = item
    segment = jnp.cumsum(starts, dtype=jnp.int32)
    first = (segment == 0).astype(jnp.bfloat16)[:, None, None]
    last = (segment == segment[-1]).astype(jnp.bfloat16)[:, None, None]
    keep = (segment[-1] == 0).astype(jnp.float32)
    query_h = queries.reshape(SPAN, H, HD).astype(jnp.float32)
    key_h = keys.reshape(SPAN, H, HD).astype(jnp.float32)
    value_h = values.reshape(SPAN, H, HD).astype(jnp.float32)
    grad_h = out_grad.reshape(SPAN, H, HD).astype(jnp.float32)
    fwd_local = jnp.einsum("thd,the->hde", key_h * last.astype(jnp.float32), value_h)
    bwd_local = jnp.einsum("thd,the->hde", query_h * first.astype(jnp.float32), grad_h)
    return keep, fwd_local, bwd_local


def block_grads(item):
    queries, keys, values, out_grad, starts, fwd_in, bwd_in = item
    segment = jnp.cumsum(starts, dtype=jnp.int32)
    position = jnp.arange(SPAN, dtype=jnp.int32)
    allowed = (position[None, :] <= position[:, None]) & (segment[:, None] == segment[None, :])
    first = (segment == 0).astype(jnp.float32)[:, None, None]
    last = (segment == segment[-1]).astype(jnp.float32)[:, None, None]
    query_h = queries.reshape(SPAN, H, HD).astype(jnp.float32)
    key_h = keys.reshape(SPAN, H, HD).astype(jnp.float32)
    value_h = values.reshape(SPAN, H, HD).astype(jnp.float32)
    grad_h = out_grad.reshape(SPAN, H, HD).astype(jnp.float32)
    score_ov = jnp.where(allowed[None], jnp.einsum("thd,shd->hts", grad_h, value_h), 0.0).astype(jnp.bfloat16).astype(jnp.float32)
    score_qk = jnp.where(allowed[None], jnp.einsum("thd,shd->hts", query_h, key_h), 0.0).astype(jnp.bfloat16).astype(jnp.float32)
    fwd_b = fwd_in.astype(jnp.bfloat16).astype(jnp.float32)
    bwd_b = bwd_in.astype(jnp.bfloat16).astype(jnp.float32)
    grad_q = jnp.einsum("hts,shd->thd", score_ov, key_h) + first * jnp.einsum("the,hde->thd", grad_h, fwd_b)
    grad_k = jnp.einsum("hts,thd->shd", score_ov, query_h) + last * jnp.einsum("the,hde->thd", value_h, bwd_b)
    grad_v = jnp.einsum("hts,thd->shd", score_qk, grad_h) + last * jnp.einsum("thd,hde->the", key_h, bwd_b)
    width = H * HD
    return (grad_q.reshape(SPAN, width).astype(jnp.bfloat16), grad_k.reshape(SPAN, width).astype(jnp.bfloat16), grad_v.reshape(SPAN, width).astype(jnp.bfloat16))


def chain_step(carry, item):
    keep, state = item
    return state + keep * carry, carry


def reference(queries, keys, values, out_grad, starts, owners):
    width = H * HD
    blocks = (queries.reshape(N_SEQ, SPAN, width), keys.reshape(N_SEQ, SPAN, width), values.reshape(N_SEQ, SPAN, width), out_grad.reshape(N_SEQ, SPAN, width), starts.reshape(N_SEQ, SPAN))
    keep, fwd_local, bwd_local = lax.map(block_states, blocks)
    zeros = jnp.zeros((H, HD, HD), jnp.float32)
    unused, fwd_in = lax.scan(chain_step, zeros, (keep, fwd_local))
    unused, bwd_in = lax.scan(chain_step, zeros, (keep, bwd_local), reverse=True)
    grad_q, grad_k, grad_v = lax.map(block_grads, blocks + (fwd_in, bwd_in))
    stacked = jnp.stack([grad_q.reshape(TOKENS, width), grad_k.reshape(TOKENS, width), grad_v.reshape(TOKENS, width)], axis=1)
    owner_ids = owners[:, 0].reshape(N_SEQ, SPAN).astype(jnp.int32)
    onehot = (owner_ids[:, :, None] == jnp.arange(N_HEAD, dtype=jnp.int32)[None, None, :]).astype(jnp.int32)
    before = jnp.cumsum(onehot, axis=1, dtype=jnp.int32) - onehot
    slots = jnp.sum(before * onehot, axis=2).astype(jnp.int32)
    block_index = jnp.arange(N_SEQ, dtype=jnp.int32)[:, None]
    target = ((block_index * N_HEAD + owner_ids) * CAP + slots).reshape(TOKENS).astype(jnp.int32)
    returned = jnp.zeros((N_SEQ * N_HEAD * CAP, 3, width), jnp.bfloat16).at[target].set(stacked)
    return returned
```

```python
import functools

import jax
import jax.numpy as jnp
from jax import lax
from jax.experimental import pallas as pl
from jax.experimental.pallas import tpu as pltpu
from jax.sharding import PartitionSpec as P

HD = 128
TILE = 256
F32 = jnp.float32
BF16 = jnp.bfloat16
VMEM_BYTES = 32 << 20


def dot_nn(a, b):
    return lax.dot_general(a, b, (((1,), (0,)), ((), ())), preferred_element_type=F32)


def dot_nt(a, b):
    return lax.dot_general(a, b, (((1,), (1,)), ((), ())), preferred_element_type=F32)


def dot_tn(a, b):
    return lax.dot_general(a, b, (((0,), (0,)), ((), ())), preferred_element_type=F32)


def params(steps=1):
    return pltpu.CompilerParams(
        dimension_semantics=("arbitrary",) * steps, vmem_limit_bytes=VMEM_BYTES
    )


def states_body(count, capacity, starts, owners, q, k, v, g, pay, seg_row, seg_col, dest):
    span = starts.shape[1]

    @pl.when(pl.program_id(0) == 0)
    def _():
        begin = starts[...]
        owner = owners[...]
        rows = lax.broadcasted_iota(jnp.int32, (count + 8, span), 0)
        hit = jnp.where(rows < count, owner, begin) == jnp.where(rows < count, rows, 1)
        before = (
            lax.broadcasted_iota(jnp.int32, (span, span), 1)
            <= lax.broadcasted_iota(jnp.int32, (span, span), 0)
        ).astype(F32).astype(BF16)
        sums = dot_nt(hit.astype(F32).astype(BF16), before)
        seg_row[...] = sums[count:]
        mine = owner == lax.broadcasted_iota(jnp.int32, (count, span), 0)
        slot = jnp.sum(jnp.where(mine, sums[:count] - 1.0, 0.0), axis=0, keepdims=True)
        dest[...] = owner * capacity + slot.astype(jnp.int32)
        wide = jnp.broadcast_to(begin, (HD, span)).astype(F32).astype(BF16)
        seg_col[...] = dot_nt(before, wide)

    segment = seg_col[...]
    total = segment[span - 1 :, :]
    first = (segment == 0.0).astype(F32).astype(BF16)
    last = (segment == total).astype(F32).astype(BF16)
    pieces = pay.shape[0]
    part = HD // pieces
    fwd = dot_tn(k[...] * last, v[...]).astype(BF16)
    bwd = dot_tn(q[...] * first, g[...]).astype(BF16)
    pay[:, :part, :] = fwd.reshape(pieces, part, HD)
    pay[:, part : 2 * part, :] = bwd.reshape(pieces, part, HD)
    keep = (total == 0.0).astype(F32)
    pay[:, 2 * part :, :] = jnp.broadcast_to(keep[None], (pieces, 16, HD)).astype(BF16)


def chain_body(count, part, got, out):
    fwd = jnp.zeros((part, HD), F32)
    bwd = jnp.zeros((part, HD), F32)
    for turn in range(count):
        out[turn, :part, :] = fwd.astype(BF16)
        keep = got[turn, 2 * part : 2 * part + 1, :].astype(F32)
        fwd = got[turn, :part, :].astype(F32) + keep * fwd
        back = count - 1 - turn
        out[back, part:, :] = bwd.astype(BF16)
        keep = got[back, 2 * part : 2 * part + 1, :].astype(F32)
        bwd = got[back, part : 2 * part, :].astype(F32) + keep * bwd


def local_body(seg_row, seg_col, q, k, v, g, out, mask, mask_t):
    span = q.shape[0]

    @pl.when(pl.program_id(0) == 0)
    def _():
        for lo in range(0, span, TILE):
            col = seg_col[lo : lo + TILE, :1]
            same = col == seg_row[:1, :]
            here = lo + lax.broadcasted_iota(jnp.int32, (TILE, span), 0)
            there = lax.broadcasted_iota(jnp.int32, (TILE, span), 1)
            mask[lo : lo + TILE, :] = (same & (there <= here)).astype(F32).astype(BF16)
            mask_t[lo : lo + TILE, :] = (same & (there >= here)).astype(F32).astype(BF16)

    for lo in range(0, span, TILE):
        hi = lo + TILE
        score = dot_nt(g[lo:hi, :], v[:hi, :]).astype(BF16) * mask[lo:hi, :hi]
        out[0, 0, lo:hi, :] = dot_nn(score, k[:hi, :])
        score = dot_nt(v[lo:hi, :], g[lo:, :]).astype(BF16) * mask_t[lo:hi, lo:]
        out[0, 1, lo:hi, :] = dot_nn(score, q[lo:, :])
        score = dot_nt(k[lo:hi, :], q[lo:, :]).astype(BF16) * mask_t[lo:hi, lo:]
        out[0, 2, lo:hi, :] = dot_nn(score, g[lo:, :])


def send_body(part, seg_col, dest, states, local, k, v, g, out, grads):
    span = k.shape[0]
    heads = local.shape[0]
    width = heads * HD
    capacity = out.shape[2]
    owner = pl.program_id(0)

    @pl.when(owner == 0)
    def _():
        segment = seg_col[...]
        first = (segment == 0.0).astype(F32)
        last = (segment == segment[span - 1 :, :]).astype(F32)
        pieces = HD // part
        for head in range(heads):
            own = slice(head * HD, (head + 1) * HD)
            rows = slice(head * pieces, (head + 1) * pieces)
            fwd = states[rows, :part, :].reshape(HD, HD)
            bwd = states[rows, part:, :].reshape(HD, HD)
            terms = (
                first * dot_nt(g[:, own], fwd),
                last * dot_nt(v[:, own], bwd),
                last * dot_nn(k[:, own], bwd),
            )
            for kind in range(3):
                at = kind * width + head * HD
                grads[:, at : at + HD] = (local[head, kind] + terms[kind]).astype(BF16)

    slots = owner * capacity + lax.broadcasted_iota(jnp.int32, (capacity, span), 0)
    pick = (dest[...] == slots).astype(F32).astype(BF16)
    rows = dot_nn(pick, grads[...]).astype(BF16)
    for kind in range(3):
        out[0, kind] = rows[:, kind * width : (kind + 1) * width]


def unpack_body(*refs):
    got, out = refs[0], refs[-1]
    out[...] = got[0]


def shards(chunks, queries, keys, values, out_grad, starts, owners):
    span, feats = queries.shape
    heads = feats // HD
    n_seq = lax.axis_size("seq")
    count = lax.axis_size("head")
    capacity = 2 * span // count
    part = heads * HD // n_seq
    pieces = HD // part
    full = lambda *shape: pl.BlockSpec(shape, lambda i: (0,) * len(shape))
    by_head = pl.BlockSpec((span, HD), lambda i: (0, i))
    starts_row = starts.reshape(1, span)
    owners_row = owners.reshape(1, span)

    payload, seg_row, seg_col, dest = pl.pallas_call(
        functools.partial(states_body, count, capacity),
        grid=(heads,),
        in_specs=[full(1, span), full(1, span)] + [by_head] * 4,
        out_specs=[
            pl.BlockSpec((pieces, 2 * part + 16, HD), lambda i: (i, 0, 0)),
            full(8, span),
            full(span, HD),
            full(1, span),
        ],
        out_shape=[
            jax.ShapeDtypeStruct((n_seq, 2 * part + 16, HD), BF16),
            jax.ShapeDtypeStruct((8, span), F32),
            jax.ShapeDtypeStruct((span, HD), F32),
            jax.ShapeDtypeStruct((1, span), jnp.int32),
        ],
        compiler_params=params(),
        name="states",
    )(starts_row, owners_row, queries, keys, values, out_grad)

    gathered = lax.all_to_all(payload, "seq", 0, 0, tiled=True)

    local = pl.pallas_call(
        local_body,
        grid=(heads,),
        in_specs=[full(8, span), full(span, HD)] + [by_head] * 4,
        out_specs=pl.BlockSpec((1, 3, span, HD), lambda i: (i, 0, 0, 0)),
        out_shape=jax.ShapeDtypeStruct((heads, 3, span, HD), F32),
        scratch_shapes=[pltpu.VMEM((span, span), BF16)] * 2,
        compiler_params=params(),
        cost_estimate=pl.CostEstimate(
            flops=heads * 8 * span * span * HD, bytes_accessed=10 << 20, transcendentals=0
        ),
        name="local",
    )(seg_row, seg_col, queries, keys, values, out_grad)

    chained = pl.pallas_call(
        functools.partial(chain_body, n_seq, part),
        out_shape=jax.ShapeDtypeStruct((n_seq, 2 * part, HD), BF16),
        compiler_params=params(0),
        name="chain",
    )(gathered)

    states = lax.all_to_all(chained, "seq", 0, 0, tiled=True)

    some = heads // chunks
    width = some * HD
    received = []
    for chunk in range(chunks):
        cols = pl.BlockSpec((span, width), lambda i, c=chunk: (0, c))
        buffer = pl.pallas_call(
            functools.partial(send_body, part),
            grid=(count,),
            in_specs=[
                full(span, HD),
                full(1, span),
                pl.BlockSpec((some * pieces, 2 * part, HD), lambda i, c=chunk: (c, 0, 0)),
                pl.BlockSpec((some, 3, span, HD), lambda i, c=chunk: (c, 0, 0, 0)),
                cols,
                cols,
                cols,
            ],
            out_specs=pl.BlockSpec((1, 3, capacity, width), lambda i: (i, 0, 0, 0)),
            out_shape=jax.ShapeDtypeStruct((count, 3, capacity, width), BF16),
            scratch_shapes=[pltpu.VMEM((span, 3 * width), BF16)],
            compiler_params=params(),
            cost_estimate=pl.CostEstimate(
                flops=2 * count * capacity * span * 3 * width,
                bytes_accessed=10 << 20,
                transcendentals=0,
            ),
            name="send",
        )(seg_col, dest, states, local, keys, values, out_grad)
        received.append(lax.all_to_all(buffer, "head", 0, 0, tiled=True))

    result = None
    for chunk in range(chunks):
        earlier = [] if result is None else [result]
        result = pl.pallas_call(
            unpack_body,
            grid=(count,),
            in_specs=[pl.BlockSpec((1, 3, capacity, width), lambda i: (i, 0, 0, 0))]
            + [pl.BlockSpec(memory_space=pl.ANY)] * len(earlier),
            out_specs=pl.BlockSpec(
                (3, capacity, width), lambda i, c=chunk: (0, 0, i * chunks + c)
            ),
            out_shape=jax.ShapeDtypeStruct((3, capacity, count * feats), BF16),
            input_output_aliases={1: 0} if earlier else {},
            compiler_params=params(),
            name="unpack",
        )(received[chunk], *earlier)
    return jnp.transpose(result, (1, 0, 2))


def solution(mesh):
    in_specs = (
        P("seq", "head"),
        P("seq", "head"),
        P("seq", "head"),
        P("seq", "head"),
        P("seq"),
        P("seq", None),
    )
    out_specs = P(("seq", "head"), None, None)
    return jax.shard_map(
        functools.partial(shards, 2),
        mesh=mesh,
        in_specs=in_specs,
        out_specs=out_specs,
        check_vma=False,
    )
```

```python
import functools

import jax
import jax.numpy as jnp
from jax import lax
from jax.experimental import pallas as pl
from jax.experimental.pallas import tpu as pltpu
from jax.sharding import PartitionSpec as P

HD = 128
TILE = 256
F32 = jnp.float32
BF16 = jnp.bfloat16


def dot_nn(a, b):
    return lax.dot_general(a, b, (((1,), (0,)), ((), ())), preferred_element_type=F32)


def dot_nt(a, b):
    return lax.dot_general(a, b, (((1,), (1,)), ((), ())), preferred_element_type=F32)


def dot_tn(a, b):
    return lax.dot_general(a, b, (((0,), (0,)), ((), ())), preferred_element_type=F32)


def params(steps=1, mebibytes=24):
    return pltpu.CompilerParams(
        dimension_semantics=("arbitrary",) * steps, vmem_limit_bytes=mebibytes << 20
    )


def states_body(count, capacity, starts, owners, q, k, v, g, pay, seg_row, seg_col, dest):
    span = starts.shape[1]

    @pl.when(pl.program_id(0) == 0)
    def _():
        begin = starts[...]
        owner = owners[...]
        rows = lax.broadcasted_iota(jnp.int32, (count + 8, span), 0)
        hit = jnp.where(rows < count, owner, begin) == jnp.where(rows < count, rows, 1)
        hit = hit.astype(F32)
        lanes = range(0, span, HD)
        stack = jnp.concatenate([hit[:, at : at + HD] for at in lanes], axis=0).astype(BF16)
        before = (
            lax.broadcasted_iota(jnp.int32, (HD, HD), 0)
            <= lax.broadcasted_iota(jnp.int32, (HD, HD), 1)
        ).astype(F32).astype(BF16)
        inner = dot_nn(stack, before)
        whole = dot_nn(stack, jnp.ones((HD, HD), BF16))
        offset = jnp.zeros((count + 8, HD), F32)
        for turn, at in enumerate(lanes):
            mine = slice(turn * (count + 8), (turn + 1) * (count + 8))
            sums = inner[mine] + offset
            offset = offset + whole[mine]
            seg_row[:, at : at + HD] = sums[count:]
            slot = jnp.sum(
                hit[:count, at : at + HD] * (sums[:count] - 1.0), axis=0, keepdims=True
            )
            dest[:, at : at + HD] = owner[:, at : at + HD] * capacity + slot.astype(jnp.int32)
            seg_col[at : at + HD, :] = jnp.broadcast_to(sums[count : count + 1], (HD, HD)).T

    segment = seg_col[...]
    total = segment[span - 1 :, :]
    first = (segment == 0.0).astype(F32).astype(BF16)
    last = (segment == total).astype(F32).astype(BF16)
    pieces = pay.shape[0]
    part = HD // pieces
    fwd = dot_tn(k[...] * last, v[...]).astype(BF16)
    bwd = dot_tn(q[...] * first, g[...]).astype(BF16)
    pay[:, :part, :] = fwd.reshape(pieces, part, HD)
    pay[:, part : 2 * part, :] = bwd.reshape(pieces, part, HD)
    keep = (total == 0.0).astype(F32)
    pay[:, 2 * part :, :] = jnp.broadcast_to(keep[None], (pieces, 16, HD)).astype(BF16)


def chain_body(count, part, got, after, out):
    del after
    fwd = jnp.zeros((part, HD), F32)
    bwd = jnp.zeros((part, HD), F32)
    for turn in range(count):
        out[turn, :part, :] = fwd.astype(BF16)
        keep = got[turn, 2 * part : 2 * part + 1, :].astype(F32)
        fwd = got[turn, :part, :].astype(F32) + keep * fwd
        back = count - 1 - turn
        out[back, part:, :] = bwd.astype(BF16)
        keep = got[back, 2 * part : 2 * part + 1, :].astype(F32)
        bwd = got[back, part : 2 * part, :].astype(F32) + keep * bwd


def local_body(seg_row, seg_col, q, k, v, g, out, token, mask, mask_t):
    span = q.shape[0]
    token[...] = jnp.zeros_like(token)

    @pl.when(pl.program_id(0) == 0)
    def _():
        for lo in range(0, span, TILE):
            col = seg_col[lo : lo + TILE, :1]
            same = col == seg_row[:1, :]
            here = lo + lax.broadcasted_iota(jnp.int32, (TILE, span), 0)
            there = lax.broadcasted_iota(jnp.int32, (TILE, span), 1)
            mask[lo : lo + TILE, :] = (same & (there <= here)).astype(F32).astype(BF16)
            mask_t[lo : lo + TILE, :] = (same & (there >= here)).astype(F32).astype(BF16)

    for lo in range(0, span, TILE):
        hi = lo + TILE
        score = dot_nt(g[lo:hi, :], v[:hi, :]).astype(BF16) * mask[lo:hi, :hi]
        out[0, 0, lo:hi, :] = dot_nn(score, k[:hi, :])
        score = dot_nt(v[lo:hi, :], g[lo:, :]).astype(BF16) * mask_t[lo:hi, lo:]
        out[0, 1, lo:hi, :] = dot_nn(score, q[lo:, :])
        score = dot_nt(k[lo:hi, :], q[lo:, :]).astype(BF16) * mask_t[lo:hi, lo:]
        out[0, 2, lo:hi, :] = dot_nn(score, g[lo:, :])


def pick_rows(dest, owner, capacity):
    shape = (capacity, dest.shape[1])
    slots = owner * capacity + lax.broadcasted_iota(jnp.int32, shape, 0)
    return (dest[...] == slots).astype(F32).astype(BF16)


def edges(seg_col):
    segment = seg_col[...]
    first = (segment == 0.0).astype(F32)
    last = (segment == segment[segment.shape[0] - 1 :, :]).astype(F32)
    return first, last


def ahead_body(targets, seg_col, dest, local, k, v, g, kept, raw, pick):
    many, _, capacity, _ = kept.shape
    head = pl.program_id(0)

    @pl.when(head == 0)
    def _():
        for turn in range(many):
            pick[turn] = pick_rows(dest, targets[turn], capacity)

    first, last = edges(seg_col)
    first, last = first.astype(BF16), last.astype(BF16)
    exact = [local[0, kind] for kind in range(3)]
    high = [part.astype(BF16) for part in exact]
    low = [(part - near.astype(F32)).astype(BF16) for part, near in zip(exact, high)]
    rows = [g[...] * first, v[...] * last, k[...] * last]
    stack = jnp.concatenate(high + low + rows, axis=1)
    for turn in range(many):
        moved = dot_nn(pick[turn], stack)
        for kind in range(3):
            at = kind * HD
            kept[turn, kind] = moved[:, at : at + HD] + moved[:, 3 * HD + at : 4 * HD + at]
            raw[turn, kind] = moved[:, 6 * HD + at : 7 * HD + at].astype(BF16)


def terms_of(states, head, part, g, v, k):
    pieces = HD // part
    rows = slice(head * pieces, (head + 1) * pieces)
    fwd = states[rows, :part, :].reshape(HD, HD)
    bwd = states[rows, part:, :].reshape(HD, HD)
    return dot_nt(g, fwd), dot_nt(v, bwd), dot_nn(k, bwd)


def finish_body(part, kept_q, kept_k, kept_v, raw_q, raw_k, raw_v, states, out):
    for head in range(out.shape[2] // HD):
        own = slice(head * HD, (head + 1) * HD)
        rows = [raw[0, 0, :, own] for raw in (raw_q, raw_k, raw_v)]
        terms = terms_of(states, head, part, *rows)
        for kind, kept in enumerate((kept_q, kept_k, kept_v)):
            out[kind, :, own] = (kept[0, 0, :, own] + terms[kind]).astype(BF16)


def combine_body(part, seg_col, states, local, k, v, g, grads):
    first, last = edges(seg_col)
    terms = terms_of(states, 0, part, g[...], v[...], k[...])
    own = pl.ds(pl.multiple_of(pl.program_id(0) * HD, HD), HD)
    for kind, edge in enumerate((first, last, last)):
        grads[kind, :, own] = (local[0, kind] + edge * terms[kind]).astype(BF16)


def place_body(target, dest, grads, out):
    pick = pick_rows(dest, target[0], out.shape[1])
    for kind in range(3):
        out[kind] = dot_nn(pick, grads[kind]).astype(BF16)


def unpack_body(many, sources, *refs):
    out, held, sems, out_sems = refs[-4:]
    feats = refs[0].shape[2]
    loads = [
        pltpu.make_async_copy(refs[turn], held.at[turn], sems.at[turn]) for turn in range(many)
    ]
    for load in loads:
        load.start()
    stores = []
    for turn in range(many):
        loads[turn].wait()
        cols = pl.ds(pl.multiple_of(sources[turn] * feats, feats), feats)
        store = pltpu.make_async_copy(
            held.at[turn], out.at[:, :, cols], out_sems.at[turn]
        )
        store.start()
        stores.append(store)
    for store in stores:
        store.wait()


def shards(queries, keys, values, out_grad, starts, owners):
    span, feats = queries.shape
    heads = feats // HD
    n_seq = lax.axis_size("seq")
    count = lax.axis_size("head")
    capacity = 2 * span // count
    part = heads * HD // n_seq
    pieces = HD // part
    full = lambda *shape: pl.BlockSpec(shape, lambda i: (0,) * len(shape))
    by_head = pl.BlockSpec((span, HD), lambda i: (0, i))
    whole = pl.BlockSpec(memory_space=pltpu.VMEM)
    smem = pl.BlockSpec(memory_space=pltpu.SMEM)
    hbm = lambda array: pltpu.with_memory_space_constraint(array, pltpu.HBM)
    in_hbm = [hbm(array) for array in (queries, keys, values, out_grad)]
    starts_row = starts.reshape(1, span)
    owners_row = owners.reshape(1, span)

    payload, seg_row, seg_col, dest = pl.pallas_call(
        functools.partial(states_body, count, capacity),
        grid=(heads,),
        in_specs=[full(1, span), full(1, span)] + [by_head] * 4,
        out_specs=[
            pl.BlockSpec((pieces, 2 * part + 16, HD), lambda i: (i, 0, 0)),
            full(8, span),
            full(span, HD),
            full(1, span),
        ],
        out_shape=[
            jax.ShapeDtypeStruct((n_seq, 2 * part + 16, HD), BF16),
            jax.ShapeDtypeStruct((8, span), F32),
            jax.ShapeDtypeStruct((span, HD), F32),
            jax.ShapeDtypeStruct((1, span), jnp.int32),
        ],
        compiler_params=params(1, 60),
        name="states",
    )(starts_row, owners_row, *in_hbm)

    gathered = lax.all_to_all(payload, "seq", 0, 0, tiled=True)

    local, token = pl.pallas_call(
        local_body,
        grid=(heads,),
        in_specs=[full(8, span), full(span, HD)] + [by_head] * 4,
        out_specs=[pl.BlockSpec((1, 3, span, HD), lambda i: (i, 0, 0, 0)), full(8, HD)],
        out_shape=[
            pltpu.HBM((heads, 3, span, HD), F32),
            jax.ShapeDtypeStruct((8, HD), F32),
        ],
        scratch_shapes=[pltpu.VMEM((span, span), BF16)] * 2,
        compiler_params=params(),
        cost_estimate=pl.CostEstimate(
            flops=heads * 8 * span * span * HD, bytes_accessed=10 << 20, transcendentals=0
        ),
        name="local",
    )(seg_row, hbm(seg_col), *in_hbm)

    chained = pl.pallas_call(
        functools.partial(chain_body, n_seq, part),
        in_specs=[whole] * 2,
        out_specs=whole,
        out_shape=jax.ShapeDtypeStruct((n_seq, 2 * part, HD), BF16),
        compiler_params=params(0),
        name="chain",
    )(gathered, token)

    states = lax.all_to_all(chained, "seq", 0, 0, tiled=True)

    me = lax.axis_index("head")
    rows = count // 2
    hops = [(rows // 2, 0), (rows // 2, 1)]
    far = len(hops)
    for step in range(1, rows // 2):
        hops += [(step, 0), (rows - step, 0), (step, 1), (rows - step, 1)]
    hops += [(0, 1), (0, 0)]

    def moved(index, hop, sign):
        row = (index // 2 + sign * hop[0]) % rows
        return row * 2 + (index % 2 + hop[1]) % 2

    def scalars(*indices):
        return jnp.stack([index.astype(jnp.int32) for index in indices])

    fixed = lambda *shape: pl.BlockSpec(shape, lambda i, *t: (0,) * len(shape))
    local_block = pl.BlockSpec((1, 3, span, HD), lambda i, *t: (i, 0, 0, 0))
    raw_block = pl.BlockSpec((span, HD), lambda i, *t: (0, i))
    out_block = pl.BlockSpec((far, 3, capacity, HD), lambda i, *t: (0, 0, 0, i))
    kept, raw = pl.pallas_call(
        ahead_body,
        grid_spec=pltpu.PrefetchScalarGridSpec(
            num_scalar_prefetch=1,
            grid=(heads,),
            in_specs=[fixed(span, HD), fixed(1, span), local_block] + [raw_block] * 3,
            out_specs=[out_block, out_block],
            scratch_shapes=[pltpu.VMEM((far, capacity, span), BF16)],
        ),
        out_shape=[
            pltpu.HBM((far, 3, capacity, feats), F32),
            pltpu.HBM((far, 3, capacity, feats), BF16),
        ],
        compiler_params=params(1),
        cost_estimate=pl.CostEstimate(
            flops=2 * far * capacity * span * 9 * feats, bytes_accessed=1 << 20, transcendentals=0
        ),
        name="ahead",
    )(
        scalars(*[moved(me, hop, 1) for hop in hops[:far]]),
        hbm(seg_col),
        hbm(dest),
        hbm(local),
        *in_hbm[1:],
    )

    def finish(turn):
        blocks = [
            pl.BlockSpec((1, 1, capacity, feats), lambda i, n=turn, kind=kind: (n, kind, 0, 0))
            for kind in range(3)
        ]
        return pl.pallas_call(
            functools.partial(finish_body, part),
            grid=(1,),
            in_specs=blocks * 2 + [whole],
            out_specs=whole,
            out_shape=pltpu.VMEM((3, capacity, feats), BF16),
            compiler_params=params(),
            cost_estimate=pl.CostEstimate(
                flops=6 * capacity * feats * HD, bytes_accessed=1 << 20, transcendentals=0
            ),
            name="finish",
        )(*[hbm(kept)] * 3, *[hbm(raw)] * 3, states)

    def combine():
        return pl.pallas_call(
            functools.partial(combine_body, part),
            grid=(heads,),
            in_specs=[
                fixed(span, HD),
                pl.BlockSpec((pieces, 2 * part, HD), lambda i: (i, 0, 0)),
                local_block,
            ]
            + [raw_block] * 3,
            out_specs=whole,
            out_shape=pltpu.VMEM((3, span, feats), BF16),
            compiler_params=params(1),
            cost_estimate=pl.CostEstimate(
                flops=6 * span * feats * HD, bytes_accessed=1 << 20, transcendentals=0
            ),
            name="combine",
        )(hbm(seg_col), states, hbm(local), *in_hbm[1:])

    def place(hop, grads):
        cost = pl.CostEstimate(
            flops=2 * capacity * span * 3 * feats, bytes_accessed=1 << 20, transcendentals=0
        )
        target = scalars(moved(me, hop, 1))
        if hop == (0, 0):
            return pl.pallas_call(
                place_body,
                grid_spec=pltpu.PrefetchScalarGridSpec(
                    num_scalar_prefetch=1,
                    grid=(1,),
                    in_specs=[whole, whole],
                    out_specs=pl.BlockSpec((3, capacity, feats), lambda i, t: (0, 0, t[0])),
                ),
                out_shape=jax.ShapeDtypeStruct((3, capacity, count * feats), BF16),
                compiler_params=params(),
                cost_estimate=cost,
                name="place",
            )(target, dest, grads)
        return pl.pallas_call(
            place_body,
            in_specs=[smem, whole, whole],
            out_specs=whole,
            out_shape=pltpu.VMEM((3, capacity, feats), BF16),
            compiler_params=params(0),
            cost_estimate=cost,
            name="place",
        )(target, dest, grads)

    def sent(chunk, hop):
        return lax.ppermute(
            chunk, "head", [(index, moved(index, hop, 1)) for index in range(count)]
        )

    received = [sent(finish(turn), hop) for turn, hop in enumerate(hops[:far])]
    grads = combine()
    received += [sent(place(hop, grads), hop) for hop in hops[far:-1]]
    result = place(hops[-1], grads)
    for lo, hi in ((0, far), (far, count - 1)):
        many = hi - lo
        result = pl.pallas_call(
            functools.partial(unpack_body, many),
            in_specs=[smem] + [pl.BlockSpec(memory_space=pl.ANY)] * (many + 1),
            out_specs=pl.BlockSpec(memory_space=pl.ANY),
            out_shape=jax.ShapeDtypeStruct((3, capacity, count * feats), BF16),
            scratch_shapes=[
                pltpu.VMEM((many, 3, capacity, feats), BF16),
                pltpu.SemaphoreType.DMA((many,)),
                pltpu.SemaphoreType.DMA((many,)),
            ],
            input_output_aliases={many + 1: 0},
            compiler_params=params(0, 16),
            cost_estimate=pl.CostEstimate(flops=0, bytes_accessed=1 << 20, transcendentals=0),
            name="unpack",
        )(
            scalars(*[moved(me, hop, -1) for hop in hops[lo:hi]]),
            *[hbm(one) for one in received[lo:hi]],
            result,
        )
    return jnp.transpose(result, (1, 0, 2))


def solution(mesh):
    in_specs = (
        P("seq", "head"),
        P("seq", "head"),
        P("seq", "head"),
        P("seq", "head"),
        P("seq"),
        P("seq", None),
    )
    out_specs = P(("seq", "head"), None, None)
    return jax.shard_map(
        shards,
        mesh=mesh,
        in_specs=in_specs,
        out_specs=out_specs,
        check_vma=False,
    )
```

```python
import functools

import jax
import jax.numpy as jnp
from jax import lax
from jax.experimental import pallas as pl
from jax.experimental.pallas import tpu as pltpu
from jax.sharding import PartitionSpec as P

HD = 128
TILE = 256
F32 = jnp.float32
BF16 = jnp.bfloat16


def dot_nn(a, b):
    return lax.dot_general(a, b, (((1,), (0,)), ((), ())), preferred_element_type=F32)


def dot_nt(a, b):
    return lax.dot_general(a, b, (((1,), (1,)), ((), ())), preferred_element_type=F32)


def dot_tn(a, b):
    return lax.dot_general(a, b, (((0,), (0,)), ((), ())), preferred_element_type=F32)


def params(steps=1, mebibytes=24):
    return pltpu.CompilerParams(
        dimension_semantics=("arbitrary",) * steps, vmem_limit_bytes=mebibytes << 20
    )


def states_body(count, capacity, starts, owners, q, k, v, g, pay, seg_row, seg_col, dest):
    span = starts.shape[1]

    @pl.when(pl.program_id(0) == 0)
    def _():
        begin = starts[...]
        owner = owners[...]
        rows = lax.broadcasted_iota(jnp.int32, (count + 8, span), 0)
        hit = jnp.where(rows < count, owner, begin) == jnp.where(rows < count, rows, 1)
        hit = hit.astype(F32)
        lanes = range(0, span, HD)
        stack = jnp.concatenate([hit[:, at : at + HD] for at in lanes], axis=0).astype(BF16)
        before = (
            lax.broadcasted_iota(jnp.int32, (HD, HD), 0)
            <= lax.broadcasted_iota(jnp.int32, (HD, HD), 1)
        ).astype(F32).astype(BF16)
        inner = dot_nn(stack, before)
        whole = dot_nn(stack, jnp.ones((HD, HD), BF16))
        offset = jnp.zeros((count + 8, HD), F32)
        for turn, at in enumerate(lanes):
            mine = slice(turn * (count + 8), (turn + 1) * (count + 8))
            sums = inner[mine] + offset
            offset = offset + whole[mine]
            seg_row[:, at : at + HD] = sums[count:]
            slot = jnp.sum(
                hit[:count, at : at + HD] * (sums[:count] - 1.0), axis=0, keepdims=True
            )
            dest[:, at : at + HD] = owner[:, at : at + HD] * capacity + slot.astype(jnp.int32)
            seg_col[at : at + HD, :] = jnp.broadcast_to(sums[count : count + 1], (HD, HD)).T

    segment = seg_col[...]
    total = segment[span - 1 :, :]
    first = (segment == 0.0).astype(F32).astype(BF16)
    last = (segment == total).astype(F32).astype(BF16)
    pieces = pay.shape[0]
    part = HD // pieces
    fwd = dot_tn(k[...] * last, v[...]).astype(BF16)
    bwd = dot_tn(q[...] * first, g[...]).astype(BF16)
    pay[:, :part, :] = fwd.reshape(pieces, part, HD)
    pay[:, part : 2 * part, :] = bwd.reshape(pieces, part, HD)
    keep = (total == 0.0).astype(F32)
    pay[:, 2 * part :, :] = jnp.broadcast_to(keep[None], (pieces, 16, HD)).astype(BF16)


def chain_body(count, part, got, after, out, token):
    token[...] = after[...]
    fwd = jnp.zeros((part, HD), F32)
    bwd = jnp.zeros((part, HD), F32)
    for turn in range(count):
        out[turn, :part, :] = fwd.astype(BF16)
        keep = got[turn, 2 * part : 2 * part + 1, :].astype(F32)
        fwd = got[turn, :part, :].astype(F32) + keep * fwd
        back = count - 1 - turn
        out[back, part:, :] = bwd.astype(BF16)
        keep = got[back, 2 * part : 2 * part + 1, :].astype(F32)
        bwd = got[back, part : 2 * part, :].astype(F32) + keep * bwd


def local_body(ahead, target, after, seg_row, seg_col, dest, q, k, v, g, *refs):
    if ahead:
        out, token, kept, raw, mask, mask_t, sums, sems, pick = refs
    else:
        out, token, mask, mask_t, sums, sems = refs
    span = q.shape[0]
    turn_now = pl.program_id(0)

    @pl.when(turn_now == 0)
    def _():
        token[...] = after[...]
        shape = (TILE, TILE)
        here = lax.broadcasted_iota(jnp.int32, shape, 0)
        there = lax.broadcasted_iota(jnp.int32, shape, 1)
        for lo in range(0, span, TILE):
            hi = lo + TILE
            col = seg_col[lo:hi, :1]
            same = col == seg_row[:1, lo:hi]
            mask[lo:hi, lo:hi] = (same & (there <= here)).astype(F32).astype(BF16)
            mask_t[lo:hi, lo:hi] = (same & (there >= here)).astype(F32).astype(BF16)
            if lo:
                mask[lo:hi, :lo] = (col == seg_row[:1, :lo]).astype(F32).astype(BF16)
            if hi < span:
                mask_t[lo:hi, hi:] = (col == seg_row[:1, hi:]).astype(F32).astype(BF16)
        if ahead:
            pick[...] = pick_rows(dest, target[0], pick.shape[0])

    def add(kind, rows, term, fresh):
        if fresh:
            sums[turn_now, kind] = term
        else:
            sums[turn_now, kind, rows, :] += term

    def write(turn, kind):
        return pltpu.make_async_copy(
            sums.at[turn, kind], out.at[turn, kind], sems.at[turn, kind]
        )

    for lo in range(0, span, TILE):
        hi = lo + TILE
        score = dot_nt(g[lo:, :], v[lo:hi, :]).astype(BF16) * mask[lo:, lo:hi]
        add(0, slice(lo, span), dot_nn(score, k[lo:hi, :]), lo == 0)
    write(turn_now, 0).start()
    for kind, left, right, other in ((1, v, g, q), (2, k, q, g)):
        for hi in range(span, 0, -TILE):
            lo = hi - TILE
            score = dot_nt(left[:hi, :], right[lo:hi, :]).astype(BF16) * mask_t[:hi, lo:hi]
            add(kind, slice(0, hi), dot_nn(score, other[lo:hi, :]), hi == span)
        write(turn_now, kind).start()

    if ahead:
        first, last = edges(seg_col)
        first, last = first.astype(BF16), last.astype(BF16)
        exact = [sums[turn_now, kind] for kind in range(3)]
        high = [part.astype(BF16) for part in exact]
        low = [(part - near.astype(F32)).astype(BF16) for part, near in zip(exact, high)]
        rows = [g[...] * first, v[...] * last, k[...] * last]
        moved = dot_nn(pick[...], jnp.concatenate(high + low + rows, axis=1))
        for kind in range(3):
            at = kind * HD
            kept[kind] = moved[:, at : at + HD] + moved[:, 3 * HD + at : 4 * HD + at]
            raw[kind] = moved[:, 6 * HD + at : 7 * HD + at].astype(BF16)

    @pl.when(turn_now == pl.num_programs(0) - 1)
    def _():
        for turn in range(sums.shape[0]):
            for kind in range(3):
                write(turn, kind).wait()


def pick_rows(dest, owner, capacity):
    shape = (capacity, dest.shape[1])
    slots = owner * capacity + lax.broadcasted_iota(jnp.int32, shape, 0)
    return (dest[...] == slots).astype(F32).astype(BF16)


def edges(seg_col):
    segment = seg_col[...]
    first = (segment == 0.0).astype(F32)
    last = (segment == segment[segment.shape[0] - 1 :, :]).astype(F32)
    return first, last


def term_of(states, head, part, kind, rows):
    pieces = HD // part
    mine = slice(head * pieces, (head + 1) * pieces)
    if kind == 0:
        return dot_nt(rows, states[mine, :part, :].reshape(HD, HD))
    bwd = states[mine, part:, :].reshape(HD, HD)
    return dot_nt(rows, bwd) if kind == 1 else dot_nn(rows, bwd)


def finish_body(part, kept_q, kept_k, kept_v, raw_q, raw_k, raw_v, states, after, out, token):
    token[...] = after[...]
    for head in range(out.shape[2] // HD):
        own = slice(head * HD, (head + 1) * HD)
        pairs = ((kept_q, raw_q), (kept_k, raw_k), (kept_v, raw_v))
        for kind, (kept, raw) in enumerate(pairs):
            term = term_of(states, head, part, kind, raw[0, :, own])
            out[kind, :, own] = (kept[0, :, own] + term).astype(BF16)


def combine_body(
    part, half, target, after, seg_col, dest, states, early, late, k, v, g, grads, out, pick
):
    del after
    head = pl.program_id(0)

    @pl.when(head == 0)
    def _():
        pick[...] = pick_rows(dest, target[0], pick.shape[0])

    first, last = edges(seg_col)
    own = pl.ds(pl.multiple_of(head * HD, HD), HD)
    for kind, (edge, rows) in enumerate(((first, g), (last, v), (last, k))):
        term = term_of(states, 0, part, kind, rows[...])
        base = jnp.where(head < half, early[0, kind], late[0, kind])
        grads[kind, :, own] = (base + edge * term).astype(BF16)

    @pl.when(head >= half)
    def _():
        for kind in range(3):
            out[kind] = dot_nn(pick[...], grads[kind, :, own]).astype(BF16)


def place_body(lo, target, dest, grads, *refs):
    out = refs[-1]
    pick = pick_rows(dest, target[0], out.shape[1])
    for kind in range(3):
        out[kind] = dot_nn(pick, grads[kind, :, lo:]).astype(BF16)


def unpack_body(feats, starts, sources, *refs):
    many = len(starts)
    out, sems, out_sems = refs[many + 1 : many + 4]
    held = refs[many + 4 :]
    loads, stores = [], []
    for turn in range(many):
        loads.append(pltpu.make_async_copy(refs[turn], held[turn], sems.at[turn]))
        loads[-1].start()
    for turn, lo in enumerate(starts):
        loads[turn].wait()
        width = held[turn].shape[2]
        cols = pl.ds(pl.multiple_of(sources[turn] * feats + lo, HD), width)
        stores.append(
            pltpu.make_async_copy(held[turn], out.at[:, :, cols], out_sems.at[turn])
        )
        stores[-1].start()
    for store in stores:
        store.wait()


def shards(queries, keys, values, out_grad, starts, owners):
    span, feats = queries.shape
    heads = feats // HD
    n_seq = lax.axis_size("seq")
    count = lax.axis_size("head")
    capacity = 2 * span // count
    part = heads * HD // n_seq
    pieces = HD // part
    full = lambda *shape: pl.BlockSpec(shape, lambda i: (0,) * len(shape))
    by_head = pl.BlockSpec((span, HD), lambda i: (0, i))
    whole = pl.BlockSpec(memory_space=pltpu.VMEM)
    smem = pl.BlockSpec(memory_space=pltpu.SMEM)
    hbm = lambda array: pltpu.with_memory_space_constraint(array, pltpu.HBM)
    in_hbm = [hbm(array) for array in (queries, keys, values, out_grad)]
    starts_row = starts.reshape(1, span)
    owners_row = owners.reshape(1, span)

    payload, seg_row, seg_col, dest = pl.pallas_call(
        functools.partial(states_body, count, capacity),
        grid=(heads,),
        in_specs=[full(1, span), full(1, span)] + [by_head] * 4,
        out_specs=[
            pl.BlockSpec((pieces, 2 * part + 16, HD), lambda i: (i, 0, 0)),
            full(8, span),
            full(span, HD),
            full(1, span),
        ],
        out_shape=[
            jax.ShapeDtypeStruct((n_seq, 2 * part + 16, HD), BF16),
            jax.ShapeDtypeStruct((8, span), F32),
            jax.ShapeDtypeStruct((span, HD), F32),
            jax.ShapeDtypeStruct((1, span), jnp.int32),
        ],
        compiler_params=params(1, 60),
        name="states",
    )(starts_row, owners_row, *in_hbm)

    gathered = lax.all_to_all(payload, "seq", 0, 0, tiled=True)

    me = lax.axis_index("head")
    rows = count // 2
    hops = [(rows // 2, 0), (rows // 2, 1)]
    far = len(hops)
    for step in range(1, rows // 2):
        hops += [(step, 0), (rows - step, 0)]
    hops += [(0, 1)]
    for step in range(1, rows // 2):
        hops += [(step, 1), (rows - step, 1)]
    hops += [(0, 0)]

    def moved(index, hop, sign):
        row = (index // 2 + sign * hop[0]) % rows
        return row * 2 + (index % 2 + hop[1]) % 2

    def scalars(*indices):
        return jnp.stack([index.astype(jnp.int32) for index in indices])

    fixed = lambda *shape: pl.BlockSpec(shape, lambda i, *t: (0,) * len(shape))
    raw_block = pl.BlockSpec((span, HD), lambda i, *t: (0, i))

    def local_half(half, after):
        base = half * (heads // 2)
        ahead = half == 0
        by = pl.BlockSpec((span, HD), lambda i, t: (0, base + i))
        block = pl.BlockSpec((3, capacity, HD), lambda i, t: (0, 0, i))
        return pl.pallas_call(
            functools.partial(local_body, ahead),
            grid_spec=pltpu.PrefetchScalarGridSpec(
                num_scalar_prefetch=1,
                grid=(heads // 2,),
                in_specs=[fixed(8, HD), fixed(8, span), fixed(span, HD), fixed(1, span)] + [by] * 4,
                out_specs=[pl.BlockSpec(memory_space=pl.ANY), fixed(8, HD)] + [block] * 2 * ahead,
                scratch_shapes=[pltpu.VMEM((span, span), BF16)] * 2
                + [
                    pltpu.VMEM((heads // 2, 3, span, HD), F32),
                    pltpu.SemaphoreType.DMA((heads // 2, 3)),
                ]
                + [pltpu.VMEM((capacity, span), BF16)] * ahead,
            ),
            out_shape=[
                pltpu.HBM((heads // 2, 3, span, HD), F32),
                jax.ShapeDtypeStruct((8, HD), F32),
            ]
            + [
                pltpu.HBM((3, capacity, feats // 2), F32),
                pltpu.HBM((3, capacity, feats // 2), BF16),
            ]
            * ahead,
            compiler_params=params(),
            cost_estimate=pl.CostEstimate(
                flops=heads * 6 * span * span * HD, bytes_accessed=10 << 20, transcendentals=0
            ),
            name="local",
        )(
            scalars(moved(me, hops[0], 1)),
            after,
            hbm(seg_row),
            hbm(seg_col),
            hbm(dest),
            *in_hbm,
        )

    early, token, kept, raw = local_half(0, hbm(seg_row))

    chained, token = pl.pallas_call(
        functools.partial(chain_body, n_seq, part),
        in_specs=[whole] * 2,
        out_specs=[whole, whole],
        out_shape=[
            jax.ShapeDtypeStruct((n_seq, 2 * part, HD), BF16),
            jax.ShapeDtypeStruct((8, HD), F32),
        ],
        compiler_params=params(0),
        name="chain",
    )(gathered, token)

    states = lax.all_to_all(chained, "seq", 0, 0, tiled=True)

    late, token = local_half(1, token)
    light = pl.CostEstimate(flops=1, bytes_accessed=1, transcendentals=0)

    blocks = [
        pl.BlockSpec((1, capacity, feats // 2), lambda i, kind=kind: (kind, 0, 0))
        for kind in range(3)
    ]
    chunk, token = pl.pallas_call(
        functools.partial(finish_body, part),
        grid=(1,),
        in_specs=blocks * 2 + [whole, whole],
        out_specs=[whole, whole],
        out_shape=[
            pltpu.VMEM((3, capacity, feats // 2), BF16),
            pltpu.VMEM((8, HD), F32),
        ],
        compiler_params=params(),
        cost_estimate=light,
        name="finish",
    )(*[hbm(kept)] * 3, *[hbm(raw)] * 3, states, token)

    def combine(after):
        half = heads // 2
        by_half = [
            pl.BlockSpec((1, 3, span, HD), lambda i, t: (jnp.minimum(i, half - 1), 0, 0, 0)),
            pl.BlockSpec((1, 3, span, HD), lambda i, t: (jnp.maximum(i - half, 0), 0, 0, 0)),
        ]
        return pl.pallas_call(
            functools.partial(combine_body, part, half),
            grid_spec=pltpu.PrefetchScalarGridSpec(
                num_scalar_prefetch=1,
                grid=(heads,),
                in_specs=[
                    whole,
                    fixed(span, HD),
                    fixed(1, span),
                    pl.BlockSpec((pieces, 2 * part, HD), lambda i, t: (i, 0, 0)),
                ]
                + by_half
                + [raw_block] * 3,
                out_specs=[
                    whole,
                    pl.BlockSpec((3, capacity, HD), lambda i, t: (0, 0, jnp.maximum(i - half, 0))),
                ],
                scratch_shapes=[pltpu.VMEM((capacity, span), BF16)],
            ),
            out_shape=[
                pltpu.VMEM((3, span, feats), BF16),
                jax.ShapeDtypeStruct((3, capacity, feats // 2), BF16),
            ],
            compiler_params=params(1),
            cost_estimate=light,
            name="combine",
        )(
            scalars(moved(me, hops[0], 1)),
            after,
            hbm(seg_col),
            hbm(dest),
            states,
            hbm(early),
            hbm(late),
            *in_hbm[1:],
        )

    def place(hop, grads, lo=0, after=()):
        later = [pl.BlockSpec(memory_space=pl.ANY)] * len(after)
        target = scalars(moved(me, hop, 1))
        if hop == (0, 0):
            return pl.pallas_call(
                functools.partial(place_body, lo),
                grid_spec=pltpu.PrefetchScalarGridSpec(
                    num_scalar_prefetch=1,
                    grid=(1,),
                    in_specs=[whole] * 2 + later,
                    out_specs=pl.BlockSpec((3, capacity, feats), lambda i, t: (0, 0, t[0])),
                ),
                out_shape=jax.ShapeDtypeStruct((3, capacity, count * feats), BF16),
                compiler_params=params(),
                cost_estimate=light,
                name="place",
            )(target, dest, grads, *after)
        return pl.pallas_call(
            functools.partial(place_body, lo),
            in_specs=[smem] + [whole] * 2 + later,
            out_specs=whole,
            out_shape=pltpu.VMEM((3, capacity, feats - lo), BF16),
            compiler_params=params(0),
            cost_estimate=light,
            name="place",
        )(target, dest, grads, *after)

    def sent(chunk, hop):
        return lax.ppermute(
            chunk, "head", [(index, moved(index, hop, 1)) for index in range(count)]
        )

    middle = feats // 2
    parts = [(hops[0], 0), (hops[0], middle)]
    received = [sent(chunk, hops[0])]
    grads, chunk = combine(token)
    received.append(sent(chunk, hops[0]))
    for hop in hops[1:-1]:
        parts.append((hop, 0))
        behind = received[0 if hops.index(hop) < far + 9 else 1]
        received.append(sent(place(hop, grads, 0, (hbm(behind),)), hop))
    result = place(hops[-1], grads, 0, (hbm(received[0]),))
    groups = ((0, far + 1), (far + 1, len(parts) - 2), (len(parts) - 2, len(parts)))
    for lo, hi in groups:
        many = hi - lo
        result = pl.pallas_call(
            functools.partial(unpack_body, feats, [start for _, start in parts[lo:hi]]),
            in_specs=[smem] + [pl.BlockSpec(memory_space=pl.ANY)] * (many + 1),
            out_specs=pl.BlockSpec(memory_space=pl.ANY),
            out_shape=jax.ShapeDtypeStruct((3, capacity, count * feats), BF16),
            scratch_shapes=[
                pltpu.SemaphoreType.DMA((many,)),
                pltpu.SemaphoreType.DMA((many,)),
            ]
            + [pltpu.VMEM(one.shape, BF16) for one in received[lo:hi]],
            input_output_aliases={many + 1: 0},
            compiler_params=params(0, 16),
            cost_estimate=light,
            name="unpack",
        )(
            scalars(*[moved(me, hop, -1) for hop, _ in parts[lo:hi]]),
            *[hbm(one) for one in received[lo:hi]],
            result,
        )
    return jnp.transpose(result, (1, 0, 2))


def solution(mesh):
    in_specs = (
        P("seq", "head"),
        P("seq", "head"),
        P("seq", "head"),
        P("seq", "head"),
        P("seq"),
        P("seq", None),
    )
    out_specs = P(("seq", "head"), None, None)
    return jax.shard_map(
        shards,
        mesh=mesh,
        in_specs=in_specs,
        out_specs=out_specs,
        check_vma=False,
    )
```

```python
import functools

import jax
import jax.numpy as jnp
from jax import lax
from jax.experimental import pallas as pl
from jax.experimental.pallas import tpu as pltpu
from jax.sharding import PartitionSpec as P

HD = 128
TILE = 256
F32 = jnp.float32
BF16 = jnp.bfloat16


def dot_nn(a, b):
    return lax.dot_general(a, b, (((1,), (0,)), ((), ())), preferred_element_type=F32)


def dot_nt(a, b):
    return lax.dot_general(a, b, (((1,), (1,)), ((), ())), preferred_element_type=F32)


def dot_tn(a, b):
    return lax.dot_general(a, b, (((0,), (0,)), ((), ())), preferred_element_type=F32)


def params(steps=1, mebibytes=24):
    return pltpu.CompilerParams(
        dimension_semantics=("arbitrary",) * steps, vmem_limit_bytes=mebibytes << 20
    )


def states_body(count, capacity, starts, owners, q, k, v, g, pay, seg_row, seg_col, dest):
    span = starts.shape[1]

    @pl.when(pl.program_id(0) == 0)
    def _():
        begin = starts[...]
        owner = owners[...]
        rows = lax.broadcasted_iota(jnp.int32, (count + 8, span), 0)
        hit = jnp.where(rows < count, owner, begin) == jnp.where(rows < count, rows, 1)
        hit = hit.astype(F32)
        lanes = range(0, span, HD)
        stack = jnp.concatenate([hit[:, at : at + HD] for at in lanes], axis=0).astype(BF16)
        before = (
            lax.broadcasted_iota(jnp.int32, (HD, HD), 0)
            <= lax.broadcasted_iota(jnp.int32, (HD, HD), 1)
        ).astype(F32).astype(BF16)
        inner = dot_nn(stack, before)
        whole = dot_nn(stack, jnp.ones((HD, HD), BF16))
        offset = jnp.zeros((count + 8, HD), F32)
        for turn, at in enumerate(lanes):
            mine = slice(turn * (count + 8), (turn + 1) * (count + 8))
            sums = inner[mine] + offset
            offset = offset + whole[mine]
            seg_row[:, at : at + HD] = sums[count:]
            slot = jnp.sum(
                hit[:count, at : at + HD] * (sums[:count] - 1.0), axis=0, keepdims=True
            )
            dest[:, at : at + HD] = owner[:, at : at + HD] * capacity + slot.astype(jnp.int32)
            seg_col[at : at + HD, :] = jnp.broadcast_to(sums[count : count + 1], (HD, HD)).T

    segment = seg_col[...]
    total = segment[span - 1 :, :]
    first = (segment == 0.0).astype(F32).astype(BF16)
    last = (segment == total).astype(F32).astype(BF16)
    pieces = pay.shape[0]
    part = HD // pieces
    fwd = dot_tn(k[...] * last, v[...]).astype(BF16)
    bwd = dot_tn(q[...] * first, g[...]).astype(BF16)
    pay[:, :part, :] = fwd.reshape(pieces, part, HD)
    pay[:, part : 2 * part, :] = bwd.reshape(pieces, part, HD)
    keep = (total == 0.0).astype(F32)
    pay[:, 2 * part :, :] = jnp.broadcast_to(keep[None], (pieces, 16, HD)).astype(BF16)


def chain_body(count, part, got, after, out, token):
    token[...] = after[...]
    fwd = jnp.zeros((part, HD), F32)
    bwd = jnp.zeros((part, HD), F32)
    for turn in range(count):
        out[turn, :part, :] = fwd.astype(BF16)
        keep = got[turn, 2 * part : 2 * part + 1, :].astype(F32)
        fwd = got[turn, :part, :].astype(F32) + keep * fwd
        back = count - 1 - turn
        out[back, part:, :] = bwd.astype(BF16)
        keep = got[back, 2 * part : 2 * part + 1, :].astype(F32)
        bwd = got[back, part : 2 * part, :].astype(F32) + keep * bwd


def local_body(ahead, target, after, seg_row, seg_col, dest, q, k, v, g, *refs):
    if ahead:
        out, token, kept, raw, mask, mask_t, sums, sems, pick = refs
        base = 0
    else:
        out, token, mask, mask_t, sums, sems = refs[1:]
        base = sums.shape[0]
    span = q.shape[0]
    turn_now = pl.program_id(0)

    @pl.when(turn_now == 0)
    def _():
        token[...] = after[...]
        shape = (TILE, TILE)
        here = lax.broadcasted_iota(jnp.int32, shape, 0)
        there = lax.broadcasted_iota(jnp.int32, shape, 1)
        for lo in range(0, span, TILE):
            hi = lo + TILE
            col = seg_col[lo:hi, :1]
            same = col == seg_row[:1, lo:hi]
            mask[lo:hi, lo:hi] = (same & (there <= here)).astype(F32).astype(BF16)
            mask_t[lo:hi, lo:hi] = (same & (there >= here)).astype(F32).astype(BF16)
            if lo:
                mask[lo:hi, :lo] = (col == seg_row[:1, :lo]).astype(F32).astype(BF16)
            if hi < span:
                mask_t[lo:hi, hi:] = (col == seg_row[:1, hi:]).astype(F32).astype(BF16)
        if ahead:
            pick[...] = pick_rows(dest, target[0], pick.shape[0])

    def add(kind, rows, term, fresh):
        if fresh:
            sums[turn_now, kind] = term
        else:
            sums[turn_now, kind, rows, :] += term

    def write(turn, kind):
        return pltpu.make_async_copy(
            sums.at[turn, kind], out.at[base + turn, kind], sems.at[turn, kind]
        )

    for lo in range(0, span, TILE):
        hi = lo + TILE
        score = dot_nt(g[lo:, :], v[lo:hi, :]).astype(BF16) * mask[lo:, lo:hi]
        add(0, slice(lo, span), dot_nn(score, k[lo:hi, :]), lo == 0)
    write(turn_now, 0).start()
    for kind, left, right, other in ((1, v, g, q), (2, k, q, g)):
        for hi in range(span, 0, -TILE):
            lo = hi - TILE
            score = dot_nt(left[:hi, :], right[lo:hi, :]).astype(BF16) * mask_t[:hi, lo:hi]
            add(kind, slice(0, hi), dot_nn(score, other[lo:hi, :]), hi == span)
        write(turn_now, kind).start()

    if ahead:
        first, last = edges(seg_col)
        first, last = first.astype(BF16), last.astype(BF16)
        exact = [sums[turn_now, kind] for kind in range(3)]
        high = [part.astype(BF16) for part in exact]
        low = [(part - near.astype(F32)).astype(BF16) for part, near in zip(exact, high)]
        rows = [g[...] * first, v[...] * last, k[...] * last]
        moved = dot_nn(pick[...], jnp.concatenate(high + low + rows, axis=1))
        for kind in range(3):
            at = kind * HD
            kept[kind] = moved[:, at : at + HD] + moved[:, 3 * HD + at : 4 * HD + at]
            raw[kind] = moved[:, 6 * HD + at : 7 * HD + at].astype(BF16)

    @pl.when(turn_now == pl.num_programs(0) - 1)
    def _():
        for turn in range(sums.shape[0]):
            for kind in range(3):
                write(turn, kind).wait()


def pick_rows(dest, owner, capacity):
    shape = (capacity, dest.shape[1])
    slots = owner * capacity + lax.broadcasted_iota(jnp.int32, shape, 0)
    return (dest[...] == slots).astype(F32).astype(BF16)


def edges(seg_col):
    segment = seg_col[...]
    first = (segment == 0.0).astype(F32)
    last = (segment == segment[segment.shape[0] - 1 :, :]).astype(F32)
    return first, last


def term_of(states, head, part, kind, rows):
    pieces = HD // part
    mine = slice(head * pieces, (head + 1) * pieces)
    if kind == 0:
        return dot_nt(rows, states[mine, :part, :].reshape(HD, HD))
    bwd = states[mine, part:, :].reshape(HD, HD)
    return dot_nt(rows, bwd) if kind == 1 else dot_nn(rows, bwd)


def finish_body(part, kept_q, kept_k, kept_v, raw_q, raw_k, raw_v, states, after, out, token):
    token[...] = after[...]
    for head in range(out.shape[2] // HD):
        own = slice(head * HD, (head + 1) * HD)
        pairs = ((kept_q, raw_q), (kept_k, raw_k), (kept_v, raw_v))
        for kind, (kept, raw) in enumerate(pairs):
            term = term_of(states, head, part, kind, raw[0, :, own])
            out[kind, :, own] = (kept[0, :, own] + term).astype(BF16)


def combine_body(
    part, half, targets, after, seg_col, dest, states, local, k, v, g, grads, rest, other, pick
):
    del after
    head = pl.program_id(0)

    @pl.when(head == 0)
    def _():
        for turn in range(2):
            pick[turn] = pick_rows(dest, targets[turn], pick.shape[1])

    first, last = edges(seg_col)
    own = pl.ds(pl.multiple_of(head * HD, HD), HD)
    for kind, (edge, rows) in enumerate(((first, g), (last, v), (last, k))):
        term = term_of(states, 0, part, kind, rows[...])
        grads[kind, :, own] = (local[0, kind] + edge * term).astype(BF16)

    now = jnp.concatenate([grads[kind, :, own] for kind in range(3)], axis=1)
    moved = dot_nn(pick[1], now).astype(BF16)
    for kind in range(3):
        other[kind] = moved[:, kind * HD : (kind + 1) * HD]

    @pl.when(head >= half)
    def _():
        moved = dot_nn(pick[0], now).astype(BF16)
        for kind in range(3):
            rest[kind] = moved[:, kind * HD : (kind + 1) * HD]


def place_body(lo, target, dest, grads, *refs):
    out = refs[-1]
    pick = pick_rows(dest, target[0], out.shape[1])
    for kind in range(3):
        out[kind] = dot_nn(pick, grads[kind, :, lo:]).astype(BF16)


def unpack_body(feats, starts, sources, *refs):
    many = len(starts)
    out, sems, out_sems = refs[many + 1 : many + 4]
    held = refs[many + 4 :]
    loads, stores = [], []
    for turn in range(many):
        loads.append(pltpu.make_async_copy(refs[turn], held[turn], sems.at[turn]))
        loads[-1].start()
    for turn, lo in enumerate(starts):
        loads[turn].wait()
        width = held[turn].shape[2]
        cols = pl.ds(pl.multiple_of(sources[turn] * feats + lo, HD), width)
        stores.append(
            pltpu.make_async_copy(held[turn], out.at[:, :, cols], out_sems.at[turn])
        )
        stores[-1].start()
    for store in stores:
        store.wait()


def shards(queries, keys, values, out_grad, starts, owners):
    span, feats = queries.shape
    heads = feats // HD
    n_seq = lax.axis_size("seq")
    count = lax.axis_size("head")
    capacity = 2 * span // count
    part = heads * HD // n_seq
    pieces = HD // part
    full = lambda *shape: pl.BlockSpec(shape, lambda i: (0,) * len(shape))
    by_head = pl.BlockSpec((span, HD), lambda i: (0, i))
    whole = pl.BlockSpec(memory_space=pltpu.VMEM)
    smem = pl.BlockSpec(memory_space=pltpu.SMEM)
    hbm = lambda array: pltpu.with_memory_space_constraint(array, pltpu.HBM)
    in_hbm = [hbm(array) for array in (queries, keys, values, out_grad)]
    starts_row = starts.reshape(1, span)
    owners_row = owners.reshape(1, span)

    payload, seg_row, seg_col, dest = pl.pallas_call(
        functools.partial(states_body, count, capacity),
        grid=(heads,),
        in_specs=[full(1, span), full(1, span)] + [by_head] * 4,
        out_specs=[
            pl.BlockSpec((pieces, 2 * part + 16, HD), lambda i: (i, 0, 0)),
            full(8, span),
            full(span, HD),
            full(1, span),
        ],
        out_shape=[
            jax.ShapeDtypeStruct((n_seq, 2 * part + 16, HD), BF16),
            jax.ShapeDtypeStruct((8, span), F32),
            jax.ShapeDtypeStruct((span, HD), F32),
            jax.ShapeDtypeStruct((1, span), jnp.int32),
        ],
        compiler_params=params(1, 60),
        name="states",
    )(starts_row, owners_row, *in_hbm)

    gathered = lax.all_to_all(payload, "seq", 0, 0, tiled=True)

    me = lax.axis_index("head")
    rows = count // 2
    hops = [(rows // 2, 0), (rows // 2, 1)]
    far = len(hops)
    for step in range(1, rows // 2):
        hops += [(step, 0), (rows - step, 0)]
    hops += [(0, 1)]
    for step in range(1, rows // 2):
        hops += [(step, 1), (rows - step, 1)]
    hops += [(0, 0)]

    def moved(index, hop, sign):
        row = (index // 2 + sign * hop[0]) % rows
        return row * 2 + (index % 2 + hop[1]) % 2

    def scalars(*indices):
        return jnp.stack([index.astype(jnp.int32) for index in indices])

    fixed = lambda *shape: pl.BlockSpec(shape, lambda i, *t: (0,) * len(shape))
    raw_block = pl.BlockSpec((span, HD), lambda i, *t: (0, i))

    def local_half(half, after, *earlier):
        base = half * (heads // 2)
        ahead = half == 0
        by = pl.BlockSpec((span, HD), lambda i, t: (0, base + i))
        block = pl.BlockSpec((3, capacity, HD), lambda i, t: (0, 0, i))
        return pl.pallas_call(
            functools.partial(local_body, ahead),
            grid_spec=pltpu.PrefetchScalarGridSpec(
                num_scalar_prefetch=1,
                grid=(heads // 2,),
                in_specs=[fixed(8, HD), fixed(8, span), fixed(span, HD), fixed(1, span)]
                + [by] * 4
                + [pl.BlockSpec(memory_space=pl.ANY)] * len(earlier),
                out_specs=[pl.BlockSpec(memory_space=pl.ANY), fixed(8, HD)] + [block] * 2 * ahead,
                scratch_shapes=[pltpu.VMEM((span, span), BF16)] * 2
                + [
                    pltpu.VMEM((heads // 2, 3, span, HD), F32),
                    pltpu.SemaphoreType.DMA((heads // 2, 3)),
                ]
                + [pltpu.VMEM((capacity, span), BF16)] * ahead,
            ),
            out_shape=[
                pltpu.HBM((heads, 3, span, HD), F32),
                jax.ShapeDtypeStruct((8, HD), F32),
            ]
            + [
                pltpu.HBM((3, capacity, feats // 2), F32),
                pltpu.HBM((3, capacity, feats // 2), BF16),
            ]
            * ahead,
            input_output_aliases={9: 0} if earlier else {},
            compiler_params=params(),
            cost_estimate=pl.CostEstimate(
                flops=heads * 6 * span * span * HD, bytes_accessed=10 << 20, transcendentals=0
            ),
            name="local",
        )(
            scalars(moved(me, hops[0], 1)),
            after,
            hbm(seg_row),
            hbm(seg_col),
            hbm(dest),
            *in_hbm,
            *earlier,
        )

    early, token, kept, raw = local_half(0, hbm(seg_row))

    chained, token = pl.pallas_call(
        functools.partial(chain_body, n_seq, part),
        in_specs=[whole] * 2,
        out_specs=[whole, whole],
        out_shape=[
            jax.ShapeDtypeStruct((n_seq, 2 * part, HD), BF16),
            jax.ShapeDtypeStruct((8, HD), F32),
        ],
        compiler_params=params(0),
        name="chain",
    )(gathered, token)

    states = lax.all_to_all(chained, "seq", 0, 0, tiled=True)

    local, token = local_half(1, token, hbm(early))
    light = pl.CostEstimate(flops=1, bytes_accessed=1, transcendentals=0)

    blocks = [
        pl.BlockSpec((1, capacity, feats // 2), lambda i, kind=kind: (kind, 0, 0))
        for kind in range(3)
    ]
    chunk, token = pl.pallas_call(
        functools.partial(finish_body, part),
        grid=(1,),
        in_specs=blocks * 2 + [whole, whole],
        out_specs=[whole, whole],
        out_shape=[
            pltpu.VMEM((3, capacity, feats // 2), BF16),
            pltpu.VMEM((8, HD), F32),
        ],
        compiler_params=params(),
        cost_estimate=light,
        name="finish",
    )(*[hbm(kept)] * 3, *[hbm(raw)] * 3, states, token)

    def combine(after):
        half = heads // 2
        return pl.pallas_call(
            functools.partial(combine_body, part, half),
            grid_spec=pltpu.PrefetchScalarGridSpec(
                num_scalar_prefetch=1,
                grid=(heads,),
                in_specs=[
                    whole,
                    fixed(span, HD),
                    fixed(1, span),
                    pl.BlockSpec((pieces, 2 * part, HD), lambda i, t: (i, 0, 0)),
                    pl.BlockSpec((1, 3, span, HD), lambda i, t: (i, 0, 0, 0)),
                ]
                + [raw_block] * 3,
                out_specs=[
                    whole,
                    pl.BlockSpec((3, capacity, HD), lambda i, t: (0, 0, jnp.maximum(i - half, 0))),
                    pl.BlockSpec((3, capacity, HD), lambda i, t: (0, 0, i)),
                ],
                scratch_shapes=[pltpu.VMEM((2, capacity, span), BF16)],
            ),
            out_shape=[
                pltpu.VMEM((3, span, feats), BF16),
                jax.ShapeDtypeStruct((3, capacity, feats // 2), BF16),
                jax.ShapeDtypeStruct((3, capacity, feats), BF16),
            ],
            compiler_params=params(1),
            cost_estimate=light,
            name="combine",
        )(
            scalars(*[moved(me, hop, 1) for hop in hops[:2]]),
            after,
            hbm(seg_col),
            hbm(dest),
            states,
            hbm(local),
            *in_hbm[1:],
        )

    def place(hop, grads, lo=0, after=()):
        later = [pl.BlockSpec(memory_space=pl.ANY)] * len(after)
        target = scalars(moved(me, hop, 1))
        if hop == (0, 0):
            return pl.pallas_call(
                functools.partial(place_body, lo),
                grid_spec=pltpu.PrefetchScalarGridSpec(
                    num_scalar_prefetch=1,
                    grid=(1,),
                    in_specs=[whole] * 2 + later,
                    out_specs=pl.BlockSpec((3, capacity, feats), lambda i, t: (0, 0, t[0])),
                ),
                out_shape=jax.ShapeDtypeStruct((3, capacity, count * feats), BF16),
                compiler_params=params(),
                cost_estimate=light,
                name="place",
            )(target, dest, grads, *after)
        return pl.pallas_call(
            functools.partial(place_body, lo),
            in_specs=[smem] + [whole] * 2 + later,
            out_specs=whole,
            out_shape=pltpu.VMEM((3, capacity, feats - lo), BF16),
            compiler_params=params(0),
            cost_estimate=light,
            name="place",
        )(target, dest, grads, *after)

    def sent(chunk, hop):
        return lax.ppermute(
            chunk, "head", [(index, moved(index, hop, 1)) for index in range(count)]
        )

    middle = feats // 2
    parts = [(hops[0], 0), (hops[0], middle), (hops[1], 0)]
    received = [sent(chunk, hops[0])]
    grads, rest, other = combine(token)
    other, _ = lax.optimization_barrier((other, received[0]))
    received += [sent(rest, hops[0]), sent(other, hops[1])]
    for hop in hops[2:-1]:
        parts.append((hop, 0))
        received.append(sent(place(hop, grads, 0, (hbm(received[0]),)), hop))
    result = place(hops[-1], grads, 0, (hbm(received[0]),))
    groups = ((0, far + 1), (far + 1, len(parts) - 2), (len(parts) - 2, len(parts)))
    for lo, hi in groups:
        many = hi - lo
        result = pl.pallas_call(
            functools.partial(unpack_body, feats, [start for _, start in parts[lo:hi]]),
            in_specs=[smem] + [pl.BlockSpec(memory_space=pl.ANY)] * (many + 1),
            out_specs=pl.BlockSpec(memory_space=pl.ANY),
            out_shape=jax.ShapeDtypeStruct((3, capacity, count * feats), BF16),
            scratch_shapes=[
                pltpu.SemaphoreType.DMA((many,)),
                pltpu.SemaphoreType.DMA((many,)),
            ]
            + [pltpu.VMEM(one.shape, BF16) for one in received[lo:hi]],
            input_output_aliases={many + 1: 0},
            compiler_params=params(0, 16),
            cost_estimate=light,
            name="unpack",
        )(
            scalars(*[moved(me, hop, -1) for hop, _ in parts[lo:hi]]),
            *[hbm(one) for one in received[lo:hi]],
            result,
        )
    return jnp.transpose(result, (1, 0, 2))


def solution(mesh):
    in_specs = (
        P("seq", "head"),
        P("seq", "head"),
        P("seq", "head"),
        P("seq", "head"),
        P("seq"),
        P("seq", None),
    )
    out_specs = P(("seq", "head"), None, None)
    return jax.shard_map(
        shards,
        mesh=mesh,
        in_specs=in_specs,
        out_specs=out_specs,
        check_vma=False,
    )
```

```python
import functools

import jax
import jax.numpy as jnp
from jax import lax
from jax.experimental import pallas as pl
from jax.experimental.pallas import tpu as pltpu
from jax.sharding import PartitionSpec as P

HD = 128
TILE = 256
F32 = jnp.float32
BF16 = jnp.bfloat16


def dot_nn(a, b):
    return lax.dot_general(a, b, (((1,), (0,)), ((), ())), preferred_element_type=F32)


def dot_nt(a, b):
    return lax.dot_general(a, b, (((1,), (1,)), ((), ())), preferred_element_type=F32)


def dot_tn(a, b):
    return lax.dot_general(a, b, (((0,), (0,)), ((), ())), preferred_element_type=F32)


def params(steps=1, mebibytes=24):
    return pltpu.CompilerParams(
        dimension_semantics=("arbitrary",) * steps, vmem_limit_bytes=mebibytes << 20
    )


def states_body(
    count, capacity, starts, owners, q, k, v, g, pay, seg_row, seg_col, dest, fwd, bwd
):
    span = starts.shape[1]

    @pl.when(pl.program_id(0) == 0)
    def _():
        begin = starts[...]
        owner = owners[...]
        rows = lax.broadcasted_iota(jnp.int32, (count + 8, span), 0)
        hit = jnp.where(rows < count, owner, begin) == jnp.where(rows < count, rows, 1)
        hit = hit.astype(F32)
        lanes = range(0, span, HD)
        stack = jnp.concatenate([hit[:, at : at + HD] for at in lanes], axis=0).astype(BF16)
        before = (
            lax.broadcasted_iota(jnp.int32, (HD, HD), 0)
            <= lax.broadcasted_iota(jnp.int32, (HD, HD), 1)
        ).astype(F32).astype(BF16)
        inner = dot_nn(stack, before)
        whole = dot_nn(stack, jnp.ones((HD, HD), BF16))
        offset = jnp.zeros((count + 8, HD), F32)
        for turn, at in enumerate(lanes):
            mine = slice(turn * (count + 8), (turn + 1) * (count + 8))
            sums = inner[mine] + offset
            offset = offset + whole[mine]
            seg_row[:, at : at + HD] = sums[count:]
            slot = jnp.sum(
                hit[:count, at : at + HD] * (sums[:count] - 1.0), axis=0, keepdims=True
            )
            dest[:, at : at + HD] = owner[:, at : at + HD] * capacity + slot.astype(jnp.int32)
            seg_col[at : at + HD, :] = jnp.broadcast_to(sums[count : count + 1], (HD, HD)).T

        fwd[...] = jnp.zeros_like(fwd)
        bwd[...] = jnp.zeros_like(bwd)

    step = pl.program_id(0)
    size = q.shape[0]
    segment = seg_col[pl.ds(pl.multiple_of(step * size, size), size), :]
    total = seg_col[span - 1 :, :]
    first = (segment == 0.0).astype(F32).astype(BF16)
    last = (segment == total).astype(F32).astype(BF16)
    heads = fwd.shape[0]
    for head in range(heads):
        own = slice(head * HD, (head + 1) * HD)
        fwd[head] += dot_tn(k[:, own] * last, v[:, own])
        bwd[head] += dot_tn(q[:, own] * first, g[:, own])

    @pl.when(step == pl.num_programs(0) - 1)
    def _():
        pieces = pay.shape[0] // heads
        part = HD // pieces
        for head in range(heads):
            rows = slice(head * pieces, (head + 1) * pieces)
            pay[rows, :part, :] = fwd[head].astype(BF16).reshape(pieces, part, HD)
            pay[rows, part : 2 * part, :] = bwd[head].astype(BF16).reshape(pieces, part, HD)
        keep = (total == 0.0).astype(F32)
        pay[:, 2 * part :, :] = jnp.broadcast_to(
            keep[None], (pay.shape[0], pay.shape[1] - 2 * part, HD)
        ).astype(BF16)


def chain_body(count, part, got, after, out, token):
    token[...] = after[...]
    fwd = jnp.zeros((part, HD), F32)
    bwd = jnp.zeros((part, HD), F32)
    for turn in range(count):
        out[turn, :part, :] = fwd.astype(BF16)
        keep = got[turn, 2 * part : 2 * part + 1, :].astype(F32)
        fwd = got[turn, :part, :].astype(F32) + keep * fwd
        back = count - 1 - turn
        out[back, part:, :] = bwd.astype(BF16)
        keep = got[back, 2 * part : 2 * part + 1, :].astype(F32)
        bwd = got[back, part : 2 * part, :].astype(F32) + keep * bwd


def local_body(ahead, target, after, seg_row, seg_col, dest, q, k, v, g, *refs):
    if ahead:
        out, token, kept, raw, mask, mask_t, sums, sems, pick = refs
        base = 0
    else:
        out, token, mask, mask_t, sums, sems = refs[1:]
        base = sums.shape[0]
    span = q.shape[0]
    turn_now = pl.program_id(0)

    @pl.when(turn_now == 0)
    def _():
        token[...] = after[...]
        shape = (TILE, TILE)
        here = lax.broadcasted_iota(jnp.int32, shape, 0)
        there = lax.broadcasted_iota(jnp.int32, shape, 1)
        for lo in range(0, span, TILE):
            hi = lo + TILE
            col = seg_col[lo:hi, :1]
            same = col == seg_row[:1, lo:hi]
            mask[lo:hi, lo:hi] = (same & (there <= here)).astype(F32).astype(BF16)
            mask_t[lo:hi, lo:hi] = (same & (there >= here)).astype(F32).astype(BF16)
            if lo:
                mask[lo:hi, :lo] = (col == seg_row[:1, :lo]).astype(F32).astype(BF16)
            if hi < span:
                mask_t[lo:hi, hi:] = (col == seg_row[:1, hi:]).astype(F32).astype(BF16)
        if ahead:
            pick[...] = pick_rows(dest, target[0], pick.shape[0])

    def add(kind, rows, term, fresh):
        if fresh:
            sums[turn_now, kind] = term
        else:
            sums[turn_now, kind, rows, :] += term

    def write(turn, kind):
        return pltpu.make_async_copy(
            sums.at[turn, kind], out.at[base + turn, kind], sems.at[turn, kind]
        )

    for lo in range(0, span, TILE):
        hi = lo + TILE
        score = dot_nt(g[lo:, :], v[lo:hi, :]).astype(BF16) * mask[lo:, lo:hi]
        add(0, slice(lo, span), dot_nn(score, k[lo:hi, :]), lo == 0)
    write(turn_now, 0).start()
    for kind, left, right, other in ((1, v, g, q), (2, k, q, g)):
        for hi in range(span, 0, -TILE):
            lo = hi - TILE
            score = dot_nt(left[:hi, :], right[lo:hi, :]).astype(BF16) * mask_t[:hi, lo:hi]
            add(kind, slice(0, hi), dot_nn(score, other[lo:hi, :]), hi == span)
        write(turn_now, kind).start()

    if ahead:
        first, last = edges(seg_col)
        first, last = first.astype(BF16), last.astype(BF16)
        exact = [sums[turn_now, kind] for kind in range(3)]
        high = [part.astype(BF16) for part in exact]
        low = [(part - near.astype(F32)).astype(BF16) for part, near in zip(exact, high)]
        rows = [g[...] * first, v[...] * last, k[...] * last]
        moved = dot_nn(pick[...], jnp.concatenate(high + low + rows, axis=1))
        for kind in range(3):
            at = kind * HD
            kept[kind] = moved[:, at : at + HD] + moved[:, 3 * HD + at : 4 * HD + at]
            raw[kind] = moved[:, 6 * HD + at : 7 * HD + at].astype(BF16)

    @pl.when(turn_now == pl.num_programs(0) - 1)
    def _():
        for turn in range(sums.shape[0]):
            for kind in range(3):
                write(turn, kind).wait()


def pick_rows(dest, owner, capacity):
    shape = (capacity, dest.shape[1])
    slots = owner * capacity + lax.broadcasted_iota(jnp.int32, shape, 0)
    return (dest[...] == slots).astype(F32).astype(BF16)


def edges(seg_col):
    segment = seg_col[...]
    first = (segment == 0.0).astype(F32)
    last = (segment == segment[segment.shape[0] - 1 :, :]).astype(F32)
    return first, last


def term_of(states, head, part, kind, rows):
    pieces = HD // part
    mine = slice(head * pieces, (head + 1) * pieces)
    if kind == 0:
        return dot_nt(rows, states[mine, :part, :].reshape(HD, HD))
    bwd = states[mine, part:, :].reshape(HD, HD)
    return dot_nt(rows, bwd) if kind == 1 else dot_nn(rows, bwd)


def finish_body(part, kept_q, kept_k, kept_v, raw_q, raw_k, raw_v, states, after, out, token):
    token[...] = after[...]
    for head in range(out.shape[2] // HD):
        own = slice(head * HD, (head + 1) * HD)
        pairs = ((kept_q, raw_q), (kept_k, raw_k), (kept_v, raw_v))
        for kind, (kept, raw) in enumerate(pairs):
            term = term_of(states, head, part, kind, raw[0, :, own])
            out[kind, :, own] = (kept[0, :, own] + term).astype(BF16)


def combine_body(
    part, half, targets, after, seg_col, dest, states, local, k, v, g, grads, rest, other, pick
):
    del after
    head = pl.program_id(0)

    @pl.when(head == 0)
    def _():
        for turn in range(2):
            pick[turn] = pick_rows(dest, targets[turn], pick.shape[1])

    first, last = edges(seg_col)
    own = pl.ds(pl.multiple_of(head * HD, HD), HD)
    for kind, (edge, rows) in enumerate(((first, g), (last, v), (last, k))):
        term = term_of(states, 0, part, kind, rows[...])
        grads[kind, :, own] = (local[0, kind] + edge * term).astype(BF16)

    now = jnp.concatenate([grads[kind, :, own] for kind in range(3)], axis=1)
    moved = dot_nn(pick[1], now).astype(BF16)
    for kind in range(3):
        other[kind] = moved[:, kind * HD : (kind + 1) * HD]

    @pl.when(head >= half)
    def _():
        moved = dot_nn(pick[0], now).astype(BF16)
        for kind in range(3):
            rest[kind] = moved[:, kind * HD : (kind + 1) * HD]


def place_body(lo, target, dest, grads, *refs):
    out = refs[-1]
    pick = pick_rows(dest, target[0], out.shape[1])
    for kind in range(3):
        out[kind] = dot_nn(pick, grads[kind, :, lo:]).astype(BF16)


def unpack_body(feats, starts, sources, *refs):
    many = len(starts)
    out, sems, out_sems = refs[many + 1 : many + 4]
    held = refs[many + 4 :]
    loads, stores = [], []
    for turn in range(many):
        for kind in range(3):
            loads.append(
                pltpu.make_async_copy(
                    refs[turn].at[kind], held[turn].at[kind], sems.at[turn, kind]
                )
            )
            loads[-1].start()
    for turn, lo in enumerate(starts):
        width = held[turn].shape[2]
        cols = pl.ds(pl.multiple_of(sources[turn] * feats + lo, HD), width)
        for kind in range(3):
            loads[turn * 3 + kind].wait()
            stores.append(
                pltpu.make_async_copy(
                    held[turn].at[kind], out.at[kind, :, cols], out_sems.at[turn, kind]
                )
            )
            stores[-1].start()
    for store in stores:
        store.wait()


def shards(queries, keys, values, out_grad, starts, owners):
    span, feats = queries.shape
    heads = feats // HD
    n_seq = lax.axis_size("seq")
    count = lax.axis_size("head")
    capacity = 2 * span // count
    part = heads * HD // n_seq
    pieces = HD // part
    full = lambda *shape: pl.BlockSpec(shape, lambda i: (0,) * len(shape))
    by_head = pl.BlockSpec((span, HD), lambda i: (0, i))
    whole = pl.BlockSpec(memory_space=pltpu.VMEM)
    smem = pl.BlockSpec(memory_space=pltpu.SMEM)
    hbm = lambda array: pltpu.with_memory_space_constraint(array, pltpu.HBM)
    in_hbm = [hbm(array) for array in (queries, keys, values, out_grad)]
    starts_row = starts.reshape(1, span)
    owners_row = owners.reshape(1, span)

    payload, seg_row, seg_col, dest = pl.pallas_call(
        functools.partial(states_body, count, capacity),
        grid=(span // TILE,),
        in_specs=[full(1, span), full(1, span)]
        + [pl.BlockSpec((TILE, feats), lambda i: (i, 0))] * 4,
        out_specs=[
            full(n_seq, 2 * part + 8, HD),
            full(8, span),
            full(span, HD),
            full(1, span),
        ],
        out_shape=[
            jax.ShapeDtypeStruct((n_seq, 2 * part + 8, HD), BF16),
            jax.ShapeDtypeStruct((8, span), F32),
            jax.ShapeDtypeStruct((span, HD), F32),
            jax.ShapeDtypeStruct((1, span), jnp.int32),
        ],
        scratch_shapes=[pltpu.VMEM((heads, HD, HD), F32)] * 2,
        compiler_params=params(1, 60),
        name="states",
    )(starts_row, owners_row, *in_hbm)

    gathered = lax.all_to_all(payload, "seq", 0, 0, tiled=True)

    me = lax.axis_index("head")
    rows = count // 2
    hops = [(rows // 2, 0), (rows // 2, 1)]
    far = len(hops)
    for step in range(1, rows // 2):
        hops += [(step, 0), (rows - step, 0)]
    hops += [(0, 1)]
    for step in range(1, rows // 2):
        hops += [(step, 1), (rows - step, 1)]
    hops += [(0, 0)]

    def moved(index, hop, sign):
        row = (index // 2 + sign * hop[0]) % rows
        return row * 2 + (index % 2 + hop[1]) % 2

    def scalars(*indices):
        return jnp.stack([index.astype(jnp.int32) for index in indices])

    fixed = lambda *shape: pl.BlockSpec(shape, lambda i, *t: (0,) * len(shape))
    raw_block = pl.BlockSpec((span, HD), lambda i, *t: (0, i))

    def local_half(half, after, *earlier):
        base = half * (heads // 2)
        ahead = half == 0
        by = pl.BlockSpec((span, HD), lambda i, t: (0, base + i))
        block = pl.BlockSpec((3, capacity, HD), lambda i, t: (0, 0, i))
        return pl.pallas_call(
            functools.partial(local_body, ahead),
            grid_spec=pltpu.PrefetchScalarGridSpec(
                num_scalar_prefetch=1,
                grid=(heads // 2,),
                in_specs=[fixed(8, HD), fixed(8, span), fixed(span, HD), fixed(1, span)]
                + [by] * 4
                + [pl.BlockSpec(memory_space=pl.ANY)] * len(earlier),
                out_specs=[pl.BlockSpec(memory_space=pl.ANY), fixed(8, HD)] + [block] * 2 * ahead,
                scratch_shapes=[pltpu.VMEM((span, span), BF16)] * 2
                + [
                    pltpu.VMEM((heads // 2, 3, span, HD), F32),
                    pltpu.SemaphoreType.DMA((heads // 2, 3)),
                ]
                + [pltpu.VMEM((capacity, span), BF16)] * ahead,
            ),
            out_shape=[
                pltpu.HBM((heads, 3, span, HD), F32),
                jax.ShapeDtypeStruct((8, HD), F32),
            ]
            + [
                pltpu.HBM((3, capacity, feats // 2), F32),
                pltpu.HBM((3, capacity, feats // 2), BF16),
            ]
            * ahead,
            input_output_aliases={9: 0} if earlier else {},
            compiler_params=params(),
            cost_estimate=pl.CostEstimate(
                flops=heads * 6 * span * span * HD, bytes_accessed=10 << 20, transcendentals=0
            ),
            name="local",
        )(
            scalars(moved(me, hops[0], 1)),
            after,
            hbm(seg_row),
            hbm(seg_col),
            hbm(dest),
            *in_hbm,
            *earlier,
        )

    early, token, kept, raw = local_half(0, hbm(seg_row))

    chained, token = pl.pallas_call(
        functools.partial(chain_body, n_seq, part),
        in_specs=[whole] * 2,
        out_specs=[whole, whole],
        out_shape=[
            jax.ShapeDtypeStruct((n_seq, 2 * part, HD), BF16),
            jax.ShapeDtypeStruct((8, HD), F32),
        ],
        compiler_params=params(0),
        name="chain",
    )(gathered, token)

    states = lax.all_to_all(chained, "seq", 0, 0, tiled=True)

    local, token = local_half(1, token, hbm(early))
    light = pl.CostEstimate(flops=1, bytes_accessed=1, transcendentals=0)

    blocks = [
        pl.BlockSpec((1, capacity, feats // 2), lambda i, kind=kind: (kind, 0, 0))
        for kind in range(3)
    ]
    chunk, token = pl.pallas_call(
        functools.partial(finish_body, part),
        grid=(1,),
        in_specs=blocks * 2 + [whole, whole],
        out_specs=[whole, whole],
        out_shape=[
            pltpu.VMEM((3, capacity, feats // 2), BF16),
            pltpu.VMEM((8, HD), F32),
        ],
        compiler_params=params(),
        cost_estimate=light,
        name="finish",
    )(*[hbm(kept)] * 3, *[hbm(raw)] * 3, states, token)

    def combine(after):
        half = heads // 2
        return pl.pallas_call(
            functools.partial(combine_body, part, half),
            grid_spec=pltpu.PrefetchScalarGridSpec(
                num_scalar_prefetch=1,
                grid=(heads,),
                in_specs=[
                    whole,
                    fixed(span, HD),
                    fixed(1, span),
                    pl.BlockSpec((pieces, 2 * part, HD), lambda i, t: (i, 0, 0)),
                    pl.BlockSpec((1, 3, span, HD), lambda i, t: (i, 0, 0, 0)),
                ]
                + [raw_block] * 3,
                out_specs=[
                    whole,
                    pl.BlockSpec((3, capacity, HD), lambda i, t: (0, 0, jnp.maximum(i - half, 0))),
                    pl.BlockSpec((3, capacity, HD), lambda i, t: (0, 0, i)),
                ],
                scratch_shapes=[pltpu.VMEM((2, capacity, span), BF16)],
            ),
            out_shape=[
                pltpu.VMEM((3, span, feats), BF16),
                jax.ShapeDtypeStruct((3, capacity, feats // 2), BF16),
                jax.ShapeDtypeStruct((3, capacity, feats), BF16),
            ],
            compiler_params=params(1),
            cost_estimate=light,
            name="combine",
        )(
            scalars(*[moved(me, hop, 1) for hop in hops[:2]]),
            after,
            hbm(seg_col),
            hbm(dest),
            states,
            hbm(local),
            *in_hbm[1:],
        )

    def place(hop, grads, lo=0, after=()):
        later = [pl.BlockSpec(memory_space=pl.ANY)] * len(after)
        target = scalars(moved(me, hop, 1))
        if hop == (0, 0):
            return pl.pallas_call(
                functools.partial(place_body, lo),
                grid_spec=pltpu.PrefetchScalarGridSpec(
                    num_scalar_prefetch=1,
                    grid=(1,),
                    in_specs=[whole] * 2 + later,
                    out_specs=pl.BlockSpec((3, capacity, feats), lambda i, t: (0, 0, t[0])),
                ),
                out_shape=jax.ShapeDtypeStruct((3, capacity, count * feats), BF16),
                compiler_params=params(),
                cost_estimate=light,
                name="place",
            )(target, dest, grads, *after)
        return pl.pallas_call(
            functools.partial(place_body, lo),
            in_specs=[smem] + [whole] * 2 + later,
            out_specs=whole,
            out_shape=pltpu.VMEM((3, capacity, feats - lo), BF16),
            compiler_params=params(0),
            cost_estimate=light,
            name="place",
        )(target, dest, grads, *after)

    def sent(chunk, hop):
        return lax.ppermute(
            chunk, "head", [(index, moved(index, hop, 1)) for index in range(count)]
        )

    middle = feats // 2
    parts = [(hops[0], 0), (hops[0], middle), (hops[1], 0)]
    received = [sent(chunk, hops[0])]
    grads, rest, other = combine(token)
    other, _ = lax.optimization_barrier((other, received[0]))
    received += [sent(rest, hops[0]), sent(other, hops[1])]
    for hop in hops[2:-1]:
        parts.append((hop, 0))
        received.append(sent(place(hop, grads, 0, (hbm(received[0]),)), hop))
    result = place(hops[-1], grads, 0, (hbm(received[0]),))
    groups = ((0, far + 1), (far + 1, len(parts) - 2), (len(parts) - 2, len(parts)))
    for lo, hi in groups:
        many = hi - lo
        result = pl.pallas_call(
            functools.partial(unpack_body, feats, [start for _, start in parts[lo:hi]]),
            in_specs=[smem] + [pl.BlockSpec(memory_space=pl.ANY)] * (many + 1),
            out_specs=pl.BlockSpec(memory_space=pl.ANY),
            out_shape=jax.ShapeDtypeStruct((3, capacity, count * feats), BF16),
            scratch_shapes=[
                pltpu.SemaphoreType.DMA((many, 3)),
                pltpu.SemaphoreType.DMA((many, 3)),
            ]
            + [pltpu.VMEM(one.shape, BF16) for one in received[lo:hi]],
            input_output_aliases={many + 1: 0},
            compiler_params=params(0, 16),
            cost_estimate=light,
            name="unpack",
        )(
            scalars(*[moved(me, hop, -1) for hop, _ in parts[lo:hi]]),
            *[hbm(one) for one in received[lo:hi]],
            result,
        )
    return jnp.transpose(result, (1, 0, 2))


def solution(mesh):
    in_specs = (
        P("seq", "head"),
        P("seq", "head"),
        P("seq", "head"),
        P("seq", "head"),
        P("seq"),
        P("seq", None),
    )
    out_specs = P(("seq", "head"), None, None)
    return jax.shard_map(
        shards,
        mesh=mesh,
        in_specs=in_specs,
        out_specs=out_specs,
        check_vma=False,
    )
```
